32 devices in a mesh: rows: 4 (over y, x), cols: 8 (over z, core).
Axes of the slice: x: 2, y: 2, z: 4, core: 2. Of those that a mesh axis runs over, the one named last changes fastest.
Arguments:
- tokens: bfloat16 [128, 256, 256], P('rows', 'cols'), may hold values from -45 to 45
- key_bias: bfloat16 [128, 256], P('rows', 'cols'), may hold values from -3 to 250
- cotangent: bfloat16 [128, 256, 256], P('rows', 'cols'), may hold values from -6 to 6
- gain_row: float32 [256], replicated, may hold values from 0.1 to 1.9
- w_qkv_row: bfloat16 [256, 768], replicated, may hold values from -0.375 to 0.375
- w_out_row: bfloat16 [256, 256], replicated, may hold values from -0.375 to 0.375
- gain_col: float32 [256], replicated, may hold values from 0.1 to 1.9
- w_qkv_col: bfloat16 [256, 768], replicated, may hold values from -0.375 to 0.375
- w_out_col: bfloat16 [256, 256], replicated, may hold values from -0.375 to 0.375
- gain_mlp: float32 [256], replicated, may hold values from 0.1 to 1.9
- w_up: bfloat16 [256, 1024], replicated, may hold values from -0.375 to 0.375
- w_down: bfloat16 [1024, 256], replicated, may hold values from -0.1875 to 0.1875
Outputs:
- d_tokens: bfloat16 [128, 256, 256], P('rows', 'cols')
- d_gain_row: float32 [256], replicated
- d_w_qkv_row: float32 [256, 768], replicated
- d_w_out_row: float32 [256, 256], replicated
- d_gain_col: float32 [256], replicated
- d_w_qkv_col: float32 [256, 768], replicated
- d_w_out_col: float32 [256, 256], replicated
- d_gain_mlp: float32 [256], replicated
- d_w_up: float32 [256, 1024], replicated
- d_w_down: float32 [1024, 256], replicated
The draws below stay inside these ranges and needn't reach their ends.
All inputs are finite; a program needn't handle non-finite values.
Results may differ from the reference program's by a relative error of at most 0.015.
Values may be sent and summed in bfloat16 or wider, within the bound.
No kernel may reach another device: no remote copies, remote signals or barrier semaphores. Data moves between devices by JAX's collectives and lax.ppermute only.
A program may use at most 128 MiB of HBM per device.

```python
import math
import jax
import jax.numpy as jnp
from jax import lax

D = 256
HEADS = 4
FF = 1024
GRID_H = 128
GRID_W = 256
TOKENS = 32768


def draw_tokens(key, part):
    key_base, key_rows, key_chan = jax.random.split(key, 3)
    base_values = jnp.clip(jax.random.normal(key_base, (GRID_H, GRID_W, D), jnp.float32), -5.0, 5.0)
    cell_scale = jnp.exp(jax.random.uniform(key_rows, (GRID_H, GRID_W, 1), jnp.float32, math.log(0.3), math.log(3.0)))
    channel_scale = jnp.exp(jax.random.uniform(key_chan, (D,), jnp.float32, math.log(0.3), math.log(3.0)))
    return (base_values * cell_scale * channel_scale).astype(jnp.bfloat16)


def draw_key_bias(key, part):
    key_base = jax.random.fold_in(key, 0)
    result = jnp.clip(jax.random.normal(key_base, (GRID_H, GRID_W), jnp.float32), -3.0, 3.0)
    return result.astype(jnp.bfloat16)


def steps_of(stream_key, extent, shards, least, top_value):
    level = 1.0
    for axis_at, parts in shards:
        steps = jax.random.uniform(jax.random.fold_in(jax.random.fold_in(stream_key, 6), axis_at), (parts,), jnp.float32, least / len(shards), top_value / len(shards))
        level = level * jnp.repeat(jnp.exp(steps), extent[axis_at] // parts).reshape((-1,) + (1,) * (len(extent) - 1 - axis_at))
    return level


def normal_values(key, extent, deviation, bound, pieces=(), kind=jnp.bfloat16):
    factor_of = steps_of(key, extent, pieces, -0.22, 0.18) if pieces else 1.0
    values = jax.random.normal(key, extent, jnp.float32) * deviation * factor_of
    return jnp.minimum(jnp.maximum(values, -bound), bound).astype(kind)


def setup_inputs(seed: int = 0) -> dict:
    key_of = jax.random.split(jax.random.key(seed), 13)
    return {
        "tokens": draw_tokens(jax.random.fold_in(key_of[12], 71), 0),
        "key_bias": draw_key_bias(jax.random.fold_in(key_of[12], 71), 0),
        "cotangent": normal_values(key_of[2], (GRID_H, GRID_W, D), 1.0, 6.0, ((0, 4), (1, 8))),
        "gain_row": jnp.clip(1.0 + 0.18 * jax.random.normal(key_of[3], (D,), jnp.float32), 0.1, 1.9),
        "w_qkv_row": normal_values(key_of[4], (D, 3 * D), D ** -0.5, 0.375),
        "w_out_row": normal_values(key_of[5], (D, D), D ** -0.5, 0.375),
        "gain_col": jnp.clip(1.0 + 0.18 * jax.random.normal(key_of[6], (D,), jnp.float32), 0.1, 1.9),
        "w_qkv_col": normal_values(key_of[7], (D, 3 * D), D ** -0.5, 0.375),
        "w_out_col": normal_values(key_of[8], (D, D), D ** -0.5, 0.375),
        "gain_mlp": jnp.clip(1.0 + 0.18 * jax.random.normal(key_of[9], (D,), jnp.float32), 0.1, 1.9),
        "w_up": normal_values(key_of[10], (D, FF), D ** -0.5, 0.375),
        "w_down": normal_values(key_of[11], (FF, D), FF ** -0.5, 0.1875),
    }


def product(spec_text, left_op, right_op):
    return jnp.einsum(spec_text, left_op.astype(jnp.float32), right_op.astype(jnp.float32))

def layer_norm(entries, gain_vec):
    floats = entries.astype(jnp.float32)
    centred = floats - lax.optimization_barrier(jnp.mean(floats, axis=-1, keepdims=True))
    inverse = lax.rsqrt(lax.optimization_barrier(jnp.mean(centred * centred, axis=-1, keepdims=True)) + 1e-05)
    normed = centred * inverse
    return ((normed * gain_vec).astype(jnp.bfloat16), normed, inverse)

def norm_back(grad_out, normed, inverse, gain_vec):
    scaled = grad_out * gain_vec
    result = inverse * (scaled - lax.optimization_barrier(jnp.mean(scaled, axis=-1, keepdims=True)) - normed * lax.optimization_barrier(jnp.mean(scaled * normed, axis=-1, keepdims=True)))
    gain_grad = lax.optimization_barrier(jnp.sum((grad_out * normed).reshape(-1, gain_vec.shape[0]), axis=0))
    return (result, gain_grad)

def over_cells(left_op, right_op):
    left_flat = left_op.reshape(-1, left_op.shape[-1])
    right_flat = right_op.reshape(-1, right_op.shape[-1])
    return lax.dot_general(left_flat, right_flat, (((0,), (0,)), ((), ())), preferred_element_type=jnp.float32)

def times_transpose(entries, weight):
    return lax.dot_general(entries, weight, (((entries.ndim - 1,), (1,)), ((), ())), preferred_element_type=jnp.float32)

def letters(length_axis):
    if length_axis == 1:
        return ('sqhd,skhd->shqk', 'shqk,skhd->sqhd', 'shqk,sqhd->skhd')
    return ('qshd,kshd->shqk', 'shqk,kshd->qshd', 'shqk,qshd->kshd')

def split_heads(packed, head_count):
    features = packed.shape[-1] // 3
    head_shape = packed.shape[:-1] + (head_count, features // head_count)
    return tuple((packed[..., member * features:(member + 1) * features].reshape(head_shape) for member in range(3)))

def key_terms(bias_rows, length_axis):
    floats = bias_rows.astype(jnp.float32)
    if length_axis == 0:
        floats = floats.T
    return floats[:, None, None, :]

def attention_weights(query_block, key_rows, bias_terms, factor, length_axis):
    scores = product(letters(length_axis)[0], query_block, key_rows) * factor + bias_terms
    shifted = jnp.exp(scores - lax.optimization_barrier(jnp.max(scores, axis=-1, keepdims=True)))
    return shifted / lax.optimization_barrier(jnp.sum(shifted, axis=-1, keepdims=True))

def join_blocks(stacked, length_axis, features):
    if length_axis == 0:
        return stacked.reshape((-1, stacked.shape[2], features))
    reordered = jnp.moveaxis(stacked, 0, 1)
    return reordered.reshape((reordered.shape[0], -1, features))

def attend(packed, bias_rows, head_count, length_axis):
    query_rows, key_rows, value_rows = split_heads(packed, head_count)
    length = packed.shape[length_axis]
    block_len = min(length, 512)
    factor = query_rows.shape[-1] ** (-0.5)
    bias_terms = key_terms(bias_rows, length_axis)
    mixing = letters(length_axis)[1]

    def one_block(offset):
        query_block = lax.dynamic_slice_in_dim(query_rows, offset, block_len, length_axis)
        weights = attention_weights(query_block, key_rows, bias_terms, factor, length_axis)
        return product(mixing, weights.astype(jnp.bfloat16), value_rows).astype(jnp.bfloat16)
    offsets = jnp.arange(length // block_len, dtype=jnp.int32) * block_len
    return join_blocks(lax.map(one_block, offsets), length_axis, packed.shape[-1] // 3)

def attend_back(grad_out, packed, bias_rows, head_count, length_axis):
    query_rows, key_rows, value_rows = split_heads(packed, head_count)
    features = packed.shape[-1] // 3
    grad_heads = grad_out.reshape(query_rows.shape)
    length = packed.shape[length_axis]
    block_len = min(length, 512)
    factor = query_rows.shape[-1] ** (-0.5)
    bias_terms = key_terms(bias_rows, length_axis)
    score_spec, mixing, gather_spec = letters(length_axis)

    def one_block(running, offset):
        key_grad, value_grad = running
        query_block = lax.dynamic_slice_in_dim(query_rows, offset, block_len, length_axis)
        grad_block = lax.dynamic_slice_in_dim(grad_heads, offset, block_len, length_axis)
        weights = attention_weights(query_block, key_rows, bias_terms, factor, length_axis)
        weights_low = weights.astype(jnp.bfloat16)
        weight_grad = product(score_spec, grad_block, value_rows)
        centre = lax.optimization_barrier(jnp.sum(weights * weight_grad, axis=-1, keepdims=True))
        score_grad = (weights * (weight_grad - centre) * factor).astype(jnp.bfloat16)
        query_grad = product(mixing, score_grad, key_rows)
        key_grad = key_grad + product(gather_spec, score_grad, query_block)
        value_grad = value_grad + product(gather_spec, weights_low, grad_block)
        return ((key_grad, value_grad), query_grad)
    empty_grad = jnp.zeros(key_rows.shape, jnp.float32)
    offsets = jnp.arange(length // block_len, dtype=jnp.int32) * block_len
    (key_grad, value_grad), query_parts = lax.scan(one_block, (empty_grad, empty_grad), offsets)
    query_grad = join_blocks(query_parts, length_axis, features)
    flat_shape = packed.shape[:-1] + (features,)
    joined = jnp.concatenate([query_grad, key_grad.reshape(flat_shape), value_grad.reshape(flat_shape)], axis=-1)
    return joined.astype(jnp.bfloat16)

def attention_forward(inputs, bias_rows, gain_vec, w_qkv, w_out, head_count, length_axis):
    normal_in, normed, inverse = layer_norm(inputs, gain_vec)
    packed = jnp.dot(normal_in, w_qkv, preferred_element_type=jnp.float32).astype(jnp.bfloat16)
    mixed_out = attend(packed, bias_rows, head_count, length_axis)
    output = (inputs.astype(jnp.float32) + jnp.dot(mixed_out, w_out, preferred_element_type=jnp.float32)).astype(jnp.bfloat16)
    return (output, (normal_in, normed, inverse, packed, mixed_out))

def attention_backward(grad_out, saved_parts, bias_rows, gain_vec, w_qkv, w_out, head_count, length_axis):
    normal_in, normed, inverse, packed, mixed_out = saved_parts
    out_grad = over_cells(mixed_out, grad_out)
    mixed_grad = times_transpose(grad_out, w_out).astype(jnp.bfloat16)
    packed_grad = attend_back(mixed_grad, packed, bias_rows, head_count, length_axis)
    qkv_grad = over_cells(normal_in, packed_grad)
    input_grad, gain_grad = norm_back(times_transpose(packed_grad, w_qkv), normed, inverse, gain_vec)
    return ((grad_out.astype(jnp.float32) + input_grad).astype(jnp.bfloat16), (gain_grad, qkv_grad, out_grad))

def feed_backward(inputs, grad_out, gain_vec, w_up, w_down):
    normal_in, normed, inverse = layer_norm(inputs, gain_vec)
    hidden = jnp.dot(normal_in, w_up, preferred_element_type=jnp.float32)
    active, gelu_back = jax.vjp(jax.nn.gelu, hidden)
    active_low = active.astype(jnp.bfloat16)
    down_grad = over_cells(active_low, grad_out)
    hidden_grad = gelu_back(times_transpose(grad_out, w_down))[0].astype(jnp.bfloat16)
    up_grad = over_cells(normal_in, hidden_grad)
    input_grad, gain_grad = norm_back(times_transpose(hidden_grad, w_up), normed, inverse, gain_vec)
    return ((grad_out.astype(jnp.float32) + input_grad).astype(jnp.bfloat16), (gain_grad, up_grad, down_grad))

def reference(tokens, key_bias, cotangent, gain_row, w_qkv_row, w_out_row, gain_col, w_qkv_col, w_out_col, gain_mlp, w_up, w_down):
    row_group = 4
    col_group = 8
    row_blocks = GRID_H // row_group
    col_blocks = GRID_W // col_group
    token_groups = tokens.reshape(row_blocks, row_group, GRID_W, D)
    bias_groups = key_bias.reshape(row_blocks, row_group, GRID_W)

    def row_forward(inputs):
        cell_rows, cell_bias = inputs
        return attention_forward(cell_rows, cell_bias, gain_row, w_qkv_row, w_out_row, HEADS, 1)[0]
    after_rows = lax.map(row_forward, (token_groups, bias_groups)).reshape(GRID_H, GRID_W, D)
    column_cells = jnp.swapaxes(after_rows, 0, 1).reshape(col_blocks, col_group, GRID_H, D)
    column_bias = key_bias.T.reshape(col_blocks, col_group, GRID_H)
    column_grads = jnp.swapaxes(cotangent, 0, 1).reshape(col_blocks, col_group, GRID_H, D)

    def column_step(running, inputs):
        cell_cols, cell_bias, grad_out = inputs
        cell_cols = jnp.swapaxes(cell_cols, 0, 1)
        cell_bias = cell_bias.T
        grad_out = jnp.swapaxes(grad_out, 0, 1)
        after_cols, saved_parts = attention_forward(cell_cols, cell_bias, gain_col, w_qkv_col, w_out_col, HEADS, 0)
        mid_grad, feed_grads = feed_backward(after_cols, grad_out, gain_mlp, w_up, w_down)
        cell_grad, attn_grads = attention_backward(mid_grad, saved_parts, cell_bias, gain_col, w_qkv_col, w_out_col, HEADS, 0)
        running = tuple((sum_term + new_term for sum_term, new_term in zip(running, attn_grads + feed_grads)))
        return (running, jnp.swapaxes(cell_grad, 0, 1))
    column_start = (jnp.zeros((D,), jnp.float32), jnp.zeros((D, 3 * D), jnp.float32), jnp.zeros((D, D), jnp.float32), jnp.zeros((D,), jnp.float32), jnp.zeros((D, FF), jnp.float32), jnp.zeros((FF, D), jnp.float32))
    column_sums, column_out = lax.scan(column_step, column_start, (column_cells, column_bias, column_grads))
    row_grads_in = jnp.swapaxes(column_out.reshape(GRID_W, GRID_H, D), 0, 1).reshape(row_blocks, row_group, GRID_W, D)

    def row_step(running, inputs):
        cell_rows, cell_bias, grad_out = inputs
        unused, saved_parts = attention_forward(cell_rows, cell_bias, gain_row, w_qkv_row, w_out_row, HEADS, 1)
        cell_grad, attn_grads = attention_backward(grad_out, saved_parts, cell_bias, gain_row, w_qkv_row, w_out_row, HEADS, 1)
        running = tuple((sum_term + new_term for sum_term, new_term in zip(running, attn_grads)))
        return (running, cell_grad)
    row_sums, row_out = lax.scan(row_step, column_start[:3], (token_groups, bias_groups, row_grads_in))
    factor = TOKENS ** (-0.5)
    return (row_out.reshape(GRID_H, GRID_W, D), row_sums[0] * factor, row_sums[1] * factor, row_sums[2] * factor, column_sums[0] * factor, column_sums[1] * factor, column_sums[2] * factor, column_sums[3] * factor, column_sums[4] * factor, column_sums[5] * factor)
```

```python
import functools
import jax
import jax.numpy as jnp
from jax import lax
from jax.experimental import pallas as pl
from jax.experimental.pallas import tpu as pltpu
from jax.sharding import PartitionSpec as P

HEADS = 4
LANES = 128
ALL = ("rows", "cols")
BF = jnp.bfloat16
F32 = jnp.float32
VMEM_LIMIT = 56 * 1024 * 1024


def dot(a, b):
    return lax.dot_general(a, b, (((1,), (0,)), ((), ())), preferred_element_type=F32)


def dot_nt(a, b):
    return lax.dot_general(a, b, (((1,), (1,)), ((), ())), preferred_element_type=F32)


def dot_tn(a, b):
    return lax.dot_general(a, b, (((0,), (0,)), ((), ())), preferred_element_type=F32)


def norm(x):
    centred = x - jnp.mean(x, axis=-1, keepdims=True)
    inverse = lax.rsqrt(jnp.mean(centred * centred, axis=-1, keepdims=True) + 1e-05)
    return centred * inverse, inverse


def norm_back(grad, normed, inverse, gain):
    scaled = grad * gain
    return inverse * (
        scaled
        - jnp.mean(scaled, axis=-1, keepdims=True)
        - normed * jnp.mean(scaled * normed, axis=-1, keepdims=True)
    )


def head_masks(features):
    lane = lax.broadcasted_iota(jnp.int32, (1, features), 1) // (features // HEADS)
    return [(lane == h).astype(F32).astype(BF) for h in range(HEADS)]


def softmax_heads(q, k, bias, masks, factor):
    weights = []
    for mask in masks:
        s = dot_nt(q * (mask * factor), k) + bias
        e = jnp.exp(s - jnp.max(s, axis=-1, keepdims=True))
        weights.append(e * (1.0 / jnp.sum(e, axis=-1, keepdims=True)))
    return weights


def mix_heads(weights_low, v, masks):
    return dot(
        jnp.concatenate(weights_low, axis=1),
        jnp.concatenate([v * mask for mask in masks], axis=0),
    )


def heads_back(weights, weights_low, do, q, k, v, masks, factor):
    dos = [do * mask for mask in masks]
    low = []
    for h in range(HEADS):
        dp = dot_nt(dos[h], v)
        p = weights[h]
        centre = jnp.sum(p * dp, axis=-1, keepdims=True)
        low.append((p * (dp - centre) * factor).astype(BF))
    dq = dot(
        jnp.concatenate(low, axis=1), jnp.concatenate([k * mask for mask in masks], axis=0)
    )
    dk = dot_tn(
        jnp.concatenate(low, axis=0), jnp.concatenate([q * mask for mask in masks], axis=0)
    )
    dv = dot_tn(jnp.concatenate(weights_low, axis=0), jnp.concatenate(dos, axis=0))
    return dq.astype(BF), dk.astype(BF), dv.astype(BF)


def load_cells(ref, pieces):
    return jnp.concatenate([ref[s].astype(F32) for s in range(pieces)], axis=0)


def row_bias(b_ref, row, pieces, length):
    total = b_ref[0].astype(F32)
    for s in range(1, pieces):
        total = total + b_ref[s].astype(F32)
    features = total.shape[1]
    at = lax.broadcasted_iota(jnp.int32, total.shape, 0)
    parts = length // features
    return jnp.concatenate(
        [
            jnp.sum(jnp.where(at == row * parts + t, total, 0.0), axis=0, keepdims=True)
            for t in range(parts)
        ],
        axis=1,
    )


def row_forward_kernel(
    dims, x_ref, b_ref, gain_ref, wqkv_ref, wout_ref, y_ref, h_ref, qkv_ref, o_ref, p_ref
):
    r_size, c_size, wl, cpd, length, d = dims
    factor = float(d // HEADS) ** (-0.5)
    masks = head_masks(d)
    x = load_cells(x_ref, c_size)
    n, _ = norm(x)
    h = (n * gain_ref[...]).astype(BF)
    h_ref[0] = h
    qkv = dot(h, wqkv_ref[...]).astype(BF)
    qkv_ref[0] = qkv
    q, k, v = qkv[:, :d], qkv[:, d : 2 * d], qkv[:, 2 * d :]
    bias = row_bias(b_ref, pl.program_id(0), c_size, length)
    weights = softmax_heads(q, k, bias, masks, factor)
    low = [w.astype(BF) for w in weights]
    for i in range(HEADS):
        p_ref[0, i] = low[i]
    o = mix_heads(low, v, masks).astype(BF)
    o_ref[0] = o
    y = (x + dot(o, wout_ref[...])).astype(BF)
    for c in range(c_size):
        for r in range(r_size):
            at = c * wl + r * cpd
            y_ref[r * c_size + c, 0] = y[at : at + cpd]


def row_backward_kernel(
    dims, x_ref, dy_ref, qkv_ref, p_ref, gain_ref, wqkv_ref, wout_ref,
    dt_ref, dyr_ref, dqkv_ref, dg_ref,
):
    r_size, c_size, wl, cpd, length, d = dims
    factor = float(d // HEADS) ** (-0.5)
    masks = head_masks(d)
    dy = jnp.concatenate(
        [dy_ref[r * c_size + c, 0].astype(F32) for c in range(c_size) for r in range(r_size)],
        axis=0,
    )
    dy_low = dy.astype(BF)
    dyr_ref[0] = dy_low
    do = dot_nt(dy_low, wout_ref[...]).astype(BF)
    qkv = qkv_ref[0]
    q, k, v = qkv[:, :d], qkv[:, d : 2 * d], qkv[:, 2 * d :]
    low = [p_ref[0, i] for i in range(HEADS)]
    weights = [w.astype(F32) for w in low]
    dq, dk, dv = heads_back(weights, low, do, q, k, v, masks, factor)
    dqkv = jnp.concatenate([dq, dk, dv], axis=1)
    dqkv_ref[0] = dqkv
    g = dot_nt(dqkv, wqkv_ref[...])
    n, inverse = norm(load_cells(x_ref, c_size))
    dt = (dy + norm_back(g, n, inverse, gain_ref[...])).astype(BF)
    for s in range(c_size):
        dt_ref[s] = dt[s * wl : (s + 1) * wl]
    dg = jnp.sum(g * n, axis=0, keepdims=True)

    @pl.when(pl.program_id(0) == 0)
    def _():
        dg_ref[...] = dg

    @pl.when(pl.program_id(0) != 0)
    def _():
        dg_ref[...] += dg


def column_kernel(
    dims, y_ref, ct_ref, gain_ref, wqkv_ref, wout_ref, gmlp_ref, wup_ref, wdown_ref,
    dy_ref, h2_ref, dqkv_ref, o2_ref, dy2_ref, h3_ref, du_ref, act_ref, ctc_ref, dg_ref, dgm_ref,
    wire_s, x_s, ct_s, bias_s, p_s,
):
    r_size, hl, cpd, length, d, chunk = dims
    step, steps = pl.program_id(0), pl.num_programs(0)
    factor = float(d // HEADS) ** (-0.5)
    masks = head_masks(d)
    tokens = chunk * length

    @pl.when(step == 0)
    def _():
        for lanes in range(d // LANES):
            cut = slice(lanes * LANES, (lanes + 1) * LANES)
            wire_s[lanes] = y_ref[:, cut].astype(F32)
            for j in range(cpd):
                x_s[j, :, cut] = wire_s[lanes, pl.ds(j, length, stride=cpd), :]
        block = hl * cpd
        for lanes in range(d // LANES):
            cut = slice(lanes * LANES, (lanes + 1) * LANES)
            for r in range(r_size):
                wire_s[lanes, r * block : (r + 1) * block, :] = ct_ref[r, :block, cut].astype(F32)
            for j in range(cpd):
                ct_s[j, :, cut] = wire_s[lanes, pl.ds(j, length, stride=cpd), :]
        total = ct_ref[0, block:].astype(F32)
        for r in range(1, r_size):
            total = total + ct_ref[r, block:].astype(F32)
        for j in range(cpd):
            bias_s[j] = total[j : j + 1, :length]
        dg_ref[...] = jnp.zeros_like(dg_ref)
        dgm_ref[...] = jnp.zeros_like(dgm_ref)

    at = pl.ds(step * chunk, chunk)
    x = x_s[at].reshape(tokens, d)
    ct = ct_s[at].reshape(tokens, d)
    n2, r2 = norm(x)
    h2 = (n2 * gain_ref[...]).astype(BF)
    h2_ref[...] = h2
    qkv = dot(h2, wqkv_ref[...]).astype(BF)
    outs = []
    for j in range(chunk):
        part = slice(j * length, (j + 1) * length)
        q, k, v = qkv[part, :d], qkv[part, d : 2 * d], qkv[part, 2 * d :]
        weights = softmax_heads(q, k, bias_s[step * chunk + j], masks, factor)
        for i in range(HEADS):
            p_s[j, i] = weights[i]
        outs.append(mix_heads([w.astype(BF) for w in weights], v, masks))
    o2 = jnp.concatenate(outs, axis=0).astype(BF)
    o2_ref[...] = o2
    y2 = (x + dot(o2, wout_ref[...])).astype(BF).astype(F32)
    n3, r3 = norm(y2)
    h3 = (n3 * gmlp_ref[...]).astype(BF)
    h3_ref[...] = h3
    ct_low = ct.astype(BF)
    ctc_ref[...] = ct_low
    u = dot(h3, wup_ref[...])
    root = 0.7978845608028654
    square = u * u
    t = jnp.tanh(root * (u + 0.044715 * (u * square)))
    act_ref[...] = (0.5 * u * (1.0 + t)).astype(BF)
    slope = 0.5 * (1.0 + t) + 0.5 * u * (1.0 - t * t) * (root * (1.0 + 3.0 * 0.044715 * square))
    du = (dot_nt(ct_low, wdown_ref[...]) * slope).astype(BF)
    du_ref[...] = du
    g3 = dot_nt(du, wup_ref[...])
    dgm_ref[...] += jnp.sum(g3 * n3, axis=0, keepdims=True)
    dy2 = (ct + norm_back(g3, n3, r3, gmlp_ref[...])).astype(BF)
    dy2_ref[...] = dy2
    do = dot_nt(dy2, wout_ref[...]).astype(BF)
    grads = []
    for j in range(chunk):
        part = slice(j * length, (j + 1) * length)
        q, k, v = qkv[part, :d], qkv[part, d : 2 * d], qkv[part, 2 * d :]
        weights = [p_s[j, i] for i in range(HEADS)]
        low = [w.astype(BF) for w in weights]
        grads.append(
            jnp.concatenate(heads_back(weights, low, do[part], q, k, v, masks, factor), axis=1)
        )
    dqkv = jnp.concatenate(grads, axis=0)
    dqkv_ref[...] = dqkv
    g2 = dot_nt(dqkv, wqkv_ref[...])
    dg_ref[...] += jnp.sum(g2 * n2, axis=0, keepdims=True)
    dy1 = dy2.astype(F32) + norm_back(g2, n2, r2, gain_ref[...])
    x_s[at] = dy1.reshape(chunk, length, d)

    @pl.when(step == steps - 1)
    def _():
        for lanes in range(d // LANES):
            cut = slice(lanes * LANES, (lanes + 1) * LANES)
            for j in range(cpd):
                wire_s[lanes, pl.ds(j, length, stride=cpd), :] = x_s[j, :, cut]
            dy_ref[:, cut] = wire_s[lanes].astype(BF)


def whole(shape):
    return pl.BlockSpec(shape, lambda i: (0,) * len(shape))


def params():
    return pltpu.CompilerParams(
        dimension_semantics=("arbitrary",), vmem_limit_bytes=VMEM_LIMIT
    )


def row_forward(dims, rpd, recv, gain, w_qkv, w_out):
    r_size, c_size, wl, cpd, length, d = dims
    n_dev = r_size * c_size
    extra = recv.shape[1] - rpd * wl
    return pl.pallas_call(
        functools.partial(row_forward_kernel, dims),
        grid=(rpd,),
        in_specs=[
            pl.BlockSpec((c_size, wl, d), lambda i: (0, i, 0)),
            pl.BlockSpec((c_size, extra, d), lambda i: (0, rpd * wl // extra, 0)),
            whole((1, d)),
            whole((d, 3 * d)),
            whole((d, d)),
        ],
        out_specs=[
            pl.BlockSpec((n_dev, 1, cpd, d), lambda i: (0, i, 0, 0)),
            pl.BlockSpec((1, length, d), lambda i: (i, 0, 0)),
            pl.BlockSpec((1, length, 3 * d), lambda i: (i, 0, 0)),
            pl.BlockSpec((1, length, d), lambda i: (i, 0, 0)),
            pl.BlockSpec((1, HEADS, length, length), lambda i: (i, 0, 0, 0)),
        ],
        out_shape=[
            jax.ShapeDtypeStruct((n_dev, rpd, cpd, d), BF),
            jax.ShapeDtypeStruct((rpd, length, d), BF),
            jax.ShapeDtypeStruct((rpd, length, 3 * d), BF),
            jax.ShapeDtypeStruct((rpd, length, d), BF),
            jax.ShapeDtypeStruct((rpd, HEADS, length, length), BF),
        ],
        compiler_params=params(),
        name="row_forward",
    )(recv, recv, gain, w_qkv, w_out)


def row_backward(dims, rpd, recv, dy, qkv, p, gain, w_qkv, w_out):
    r_size, c_size, wl, cpd, length, d = dims
    n_dev = r_size * c_size
    return pl.pallas_call(
        functools.partial(row_backward_kernel, dims),
        grid=(rpd,),
        in_specs=[
            pl.BlockSpec((c_size, wl, d), lambda i: (0, i, 0)),
            pl.BlockSpec((n_dev, 1, cpd, d), lambda i: (0, i, 0, 0)),
            pl.BlockSpec((1, length, 3 * d), lambda i: (i, 0, 0)),
            pl.BlockSpec((1, HEADS, length, length), lambda i: (i, 0, 0, 0)),
            whole((1, d)),
            whole((d, 3 * d)),
            whole((d, d)),
        ],
        out_specs=[
            pl.BlockSpec((c_size, wl, d), lambda i: (0, i, 0)),
            pl.BlockSpec((1, length, d), lambda i: (i, 0, 0)),
            pl.BlockSpec((1, length, 3 * d), lambda i: (i, 0, 0)),
            whole((1, d)),
        ],
        out_shape=[
            jax.ShapeDtypeStruct((c_size, rpd * wl, d), BF),
            jax.ShapeDtypeStruct((rpd, length, d), BF),
            jax.ShapeDtypeStruct((rpd, length, 3 * d), BF),
            jax.ShapeDtypeStruct((1, d), F32),
        ],
        compiler_params=params(),
        name="row_backward",
    )(recv, dy, qkv, p, gain, w_qkv, w_out)


def column_stage(dims, y_wire, ct_wire, gain, w_qkv, w_out, gain_mlp, w_up, w_down):
    r_size, hl, cpd, length, d, chunk = dims
    tokens = cpd * length
    ff = w_up.shape[1]
    part = chunk * length

    def rows_of(width):
        return pl.BlockSpec((part, width), lambda i: (i, 0))

    def shape_of(width):
        return jax.ShapeDtypeStruct((tokens, width), BF)

    widths = (d, 3 * d, d, d, d, ff, ff, d)
    return pl.pallas_call(
        functools.partial(column_kernel, dims),
        grid=(cpd // chunk,),
        in_specs=[
            whole((tokens, d)),
            whole(ct_wire.shape),
            whole((1, d)),
            whole((d, 3 * d)),
            whole((d, d)),
            whole((1, d)),
            whole((d, ff)),
            whole((ff, d)),
        ],
        out_specs=[whole((tokens, d))] + [rows_of(w) for w in widths] + [whole((1, d))] * 2,
        out_shape=[shape_of(d)]
        + [shape_of(w) for w in widths]
        + [jax.ShapeDtypeStruct((1, d), F32)] * 2,
        scratch_shapes=[
            pltpu.VMEM((d // LANES, tokens, LANES), F32),
            pltpu.VMEM((cpd, length, d), F32),
            pltpu.VMEM((cpd, length, d), F32),
            pltpu.VMEM((cpd, 1, length), F32),
            pltpu.VMEM((chunk, HEADS, length, length), F32),
        ],
        compiler_params=params(),
        name="column_stage",
    )(y_wire, ct_wire, gain, w_qkv, w_out, gain_mlp, w_up, w_down)


def exchange(x, axes):
    return lax.all_to_all(x, axes, split_axis=0, concat_axis=0, tiled=True)


def wgrad(left, right, factor):
    left = left.reshape(-1, left.shape[-1])
    right = right.reshape(-1, right.shape[-1])
    return (dot_tn(left, right) * factor).astype(BF)


def total_of(rows, r_size, c_size):
    m, d = rows.shape
    part = exchange(rows, "rows").reshape(r_size, m // r_size, d)
    part = jnp.sum(part.astype(F32), axis=0).astype(BF)
    part = exchange(part, "cols").reshape(c_size, m // r_size // c_size, d)
    part = jnp.sum(part.astype(F32), axis=0).astype(BF)
    part = lax.all_gather(part, "cols", axis=0, tiled=True)
    return lax.all_gather(part, "rows", axis=0, tiled=True)


def wide(grad, d):
    return [grad[:, i * d : (i + 1) * d] for i in range(grad.shape[1] // d)]


def narrow(rows, count, d):
    return jnp.concatenate([rows[i * d : (i + 1) * d] for i in range(count)], axis=1).astype(F32)


def shards(
    tokens, key_bias, cotangent, gain_row, w_qkv_row, w_out_row,
    gain_col, w_qkv_col, w_out_col, gain_mlp, w_up, w_down,
):
    r_size, c_size = lax.axis_size("rows"), lax.axis_size("cols")
    hl, wl, d = tokens.shape
    ff = w_up.shape[1]
    rpd, cpd = hl // c_size, wl // r_size
    row_len, col_len = wl * c_size, hl * r_size
    factor = float(row_len * col_len) ** (-0.5)
    r_at, c_at = lax.axis_index("rows"), lax.axis_index("cols")
    row_dims = (r_size, c_size, wl, cpd, row_len, d)
    chunk = min(cpd, max(1, 512 // col_len))
    col_dims = (r_size, hl, cpd, col_len, d, chunk)

    place = jnp.arange(c_size)[None, :, None] == c_at
    row_extra = jnp.where(place, key_bias[:, None, :], jnp.zeros((), BF))
    row_extra = row_extra.reshape(c_size, rpd * row_len // d, d)
    pad = -row_extra.shape[1] % 8
    row_extra = jnp.pad(row_extra, ((0, 0), (0, pad), (0, 0)))
    send = jnp.concatenate([tokens.reshape(c_size, rpd * wl, d), row_extra], axis=1)
    recv = exchange(send, "cols")

    col_bias = key_bias.T.reshape(r_size, cpd, 1, hl)
    place = jnp.arange(r_size)[None, None, :, None] == r_at
    col_extra = jnp.where(place, col_bias, jnp.zeros((), BF)).reshape(r_size, cpd, col_len)
    col_extra = jnp.pad(col_extra, ((0, 0), (0, -cpd % 8), (0, d - col_len)))
    ct_send = jnp.moveaxis(cotangent.reshape(hl, r_size, cpd, d), 1, 0)
    ct_send = jnp.concatenate([ct_send.reshape(r_size, hl * cpd, d), col_extra], axis=1)
    ct_wire = exchange(ct_send, "rows")

    y_send, h1, qkv1, o1, p1 = row_forward(
        row_dims, rpd, recv, gain_row[None], w_qkv_row, w_out_row
    )
    y_wire = exchange(y_send, ALL).reshape(hl * r_size * cpd, d)
    (dy_send, h2, dqkv2, o2, dy2, h3, du, act, ct_cols, dg_col, dg_mlp) = column_stage(
        col_dims, y_wire, ct_wire, gain_col[None], w_qkv_col, w_out_col,
        gain_mlp[None], w_up, w_down,
    )
    dy_wire = exchange(dy_send.reshape(y_send.shape), ALL)

    col_parts = wide(wgrad(h2, dqkv2, factor), d)
    col_parts += [wgrad(o2, dy2, factor)]
    col_parts += wide(wgrad(h3, du, factor), d)
    col_parts += [wgrad(act, ct_cols, factor)]
    col_sums = total_of(jnp.concatenate(col_parts, axis=0), r_size, c_size)

    dt_send, dy_rows, dqkv1, dg_row = row_backward(
        row_dims, rpd, recv, dy_wire, qkv1, p1, gain_row[None], w_qkv_row, w_out_row
    )
    gains = (jnp.concatenate([dg_row, dg_col, dg_mlp], axis=0) * factor).astype(BF)
    row_parts = wide(wgrad(h1, dqkv1, factor), d)
    row_parts += [wgrad(o1, dy_rows, factor)]
    unit = 8 * r_size * c_size
    rows = 4 * d + 3
    row_parts += [jnp.pad(gains, ((0, -rows % unit), (0, 0)))]
    row_sums = total_of(jnp.concatenate(row_parts, axis=0), r_size, c_size)
    d_tokens = exchange(dt_send, "cols").reshape(hl, wl, d)

    gain_sums = row_sums[4 * d : 4 * d + 3].astype(F32)
    nff = ff // d
    return (
        d_tokens,
        gain_sums[0],
        narrow(row_sums, 3, d),
        row_sums[3 * d : 4 * d].astype(F32),
        gain_sums[1],
        narrow(col_sums, 3, d),
        col_sums[3 * d : 4 * d].astype(F32),
        gain_sums[2],
        narrow(col_sums[4 * d :], nff, d),
        col_sums[(4 + nff) * d :].astype(F32),
    )


def solution(mesh):
    cells = P("rows", "cols", None)
    in_specs = (cells, P("rows", "cols"), cells) + (P(),) * 9
    out_specs = (cells,) + (P(),) * 9
    return jax.shard_map(shards, mesh=mesh, in_specs=in_specs, out_specs=out_specs, check_vma=False)
```

```python
import functools
import jax
import jax.numpy as jnp
from jax import lax
from jax.experimental import pallas as pl
from jax.experimental.pallas import tpu as pltpu
from jax.sharding import PartitionSpec as P

HEADS = 4
LANES = 128
ALL = ("rows", "cols")
BF = jnp.bfloat16
F32 = jnp.float32
VMEM_LIMIT = 56 * 1024 * 1024


def dot(a, b):
    return lax.dot_general(a, b, (((1,), (0,)), ((), ())), preferred_element_type=F32)


def dot_nt(a, b):
    return lax.dot_general(a, b, (((1,), (1,)), ((), ())), preferred_element_type=F32)


def dot_tn(a, b):
    return lax.dot_general(a, b, (((0,), (0,)), ((), ())), preferred_element_type=F32)


def norm(x):
    centred = x - jnp.mean(x, axis=-1, keepdims=True)
    inverse = lax.rsqrt(jnp.mean(centred * centred, axis=-1, keepdims=True) + 1e-05)
    return centred * inverse, inverse


def norm_back(grad, normed, inverse, gain):
    scaled = grad * gain
    return inverse * (
        scaled
        - jnp.mean(scaled, axis=-1, keepdims=True)
        - normed * jnp.mean(scaled * normed, axis=-1, keepdims=True)
    )


def head_masks(features):
    lane = lax.broadcasted_iota(jnp.int32, (1, features), 1) // (features // HEADS)
    return [(lane == h).astype(F32).astype(BF) for h in range(HEADS)]


def softmax_heads(q, k, bias, masks, factor):
    weights = []
    for mask in masks:
        s = dot_nt(q * (mask * factor), k) + bias
        e = jnp.exp(s - jnp.max(s, axis=-1, keepdims=True))
        weights.append(e * (1.0 / jnp.sum(e, axis=-1, keepdims=True)))
    return weights


def mix_heads(weights_low, v, masks):
    return dot(
        jnp.concatenate(weights_low, axis=1),
        jnp.concatenate([v * mask for mask in masks], axis=0),
    )


def heads_back(weights, weights_low, do, q, k, v, masks, factor):
    dos = [do * mask for mask in masks]
    low = []
    for h in range(HEADS):
        dp = dot_nt(dos[h], v)
        p = weights[h]
        centre = jnp.sum(p * dp, axis=-1, keepdims=True)
        low.append((p * (dp - centre) * factor).astype(BF))
    dq = dot(
        jnp.concatenate(low, axis=1), jnp.concatenate([k * mask for mask in masks], axis=0)
    )
    dk = dot_tn(
        jnp.concatenate(low, axis=0), jnp.concatenate([q * mask for mask in masks], axis=0)
    )
    dv = dot_tn(jnp.concatenate(weights_low, axis=0), jnp.concatenate(dos, axis=0))
    return dq.astype(BF), dk.astype(BF), dv.astype(BF)


def load_cells(ref, pieces):
    return jnp.concatenate([ref[s].astype(F32) for s in range(pieces)], axis=0)


def row_bias(b_ref, row, pieces, length):
    total = b_ref[0].astype(F32)
    for s in range(1, pieces):
        total = total + b_ref[s].astype(F32)
    features = total.shape[1]
    at = lax.broadcasted_iota(jnp.int32, total.shape, 0)
    parts = length // features
    return jnp.concatenate(
        [
            jnp.sum(jnp.where(at == row * parts + t, total, 0.0), axis=0, keepdims=True)
            for t in range(parts)
        ],
        axis=1,
    )


def row_forward_kernel(
    dims, x_ref, b_ref, gain_ref, wqkv_ref, wout_ref, y_ref, qkv_ref, o_ref, p_ref
):
    r_size, c_size, wl, cpd, length, d = dims
    factor = float(d // HEADS) ** (-0.5)
    masks = head_masks(d)
    x = load_cells(x_ref, c_size)
    n, _ = norm(x)
    h = (n * gain_ref[...]).astype(BF)
    qkv = dot(h, wqkv_ref[...]).astype(BF)
    qkv_ref[0] = qkv
    q, k, v = qkv[:, :d], qkv[:, d : 2 * d], qkv[:, 2 * d :]
    bias = row_bias(b_ref, pl.program_id(0), c_size, length)
    weights = softmax_heads(q, k, bias, masks, factor)
    low = [w.astype(BF) for w in weights]
    for i in range(HEADS):
        p_ref[0, i] = low[i]
    o = mix_heads(low, v, masks).astype(BF)
    o_ref[0] = o
    y = (x + dot(o, wout_ref[...])).astype(BF)
    for c in range(c_size):
        for r in range(r_size):
            at = c * wl + r * cpd
            y_ref[r * c_size + c, 0] = y[at : at + cpd]


def store_rows(keep_ref, send_ref, parity, row, value):
    half = keep_ref.shape[0]
    for side in range(2):
        start, stop = max(row, side * half), min(row + value.shape[0], (side + 1) * half)
        if start < stop:
            piece = value[start - row : stop - row]
            to = slice(start - side * half, stop - side * half)

            @pl.when(parity == side)
            def _():
                keep_ref[to] = piece

            @pl.when(parity != side)
            def _():
                send_ref[to] = piece


def row_backward_kernel(
    dims, x_ref, dy_ref, qkv_ref, o_ref, p_ref, gain_ref, wqkv_ref, wout_ref, dgc_ref, dgm_ref,
    dt_ref, keep_ref, send_ref, dg_s, dwqkv_s, dwout_s,
):
    r_size, c_size, wl, cpd, length, d = dims
    step, steps = pl.program_id(0), pl.num_programs(0)
    factor = float(d // HEADS) ** (-0.5)
    masks = head_masks(d)

    @pl.when(step == 0)
    def _():
        dg_s[...] = jnp.zeros_like(dg_s)
        dwqkv_s[...] = jnp.zeros_like(dwqkv_s)
        dwout_s[...] = jnp.zeros_like(dwout_s)
        keep_ref[...] = jnp.zeros_like(keep_ref)
        send_ref[...] = jnp.zeros_like(send_ref)

    dy = jnp.concatenate(
        [dy_ref[r * c_size + c, 0].astype(F32) for c in range(c_size) for r in range(r_size)],
        axis=0,
    )
    dy_low = dy.astype(BF)
    do = dot_nt(dy_low, wout_ref[...]).astype(BF)
    qkv = qkv_ref[0]
    q, k, v = qkv[:, :d], qkv[:, d : 2 * d], qkv[:, 2 * d :]
    low = [p_ref[0, i] for i in range(HEADS)]
    weights = [w.astype(F32) for w in low]
    dq, dk, dv = heads_back(weights, low, do, q, k, v, masks, factor)
    dqkv = jnp.concatenate([dq, dk, dv], axis=1)
    g = dot_nt(dqkv, wqkv_ref[...])
    n, inverse = norm(load_cells(x_ref, c_size))
    h = (n * gain_ref[...]).astype(BF)
    dt = (dy + norm_back(g, n, inverse, gain_ref[...])).astype(BF)
    for s in range(c_size):
        dt_ref[s] = dt[s * wl : (s + 1) * wl]
    dg_s[...] += jnp.sum(g * n, axis=0, keepdims=True)
    dwqkv_s[...] += dot_tn(h, dqkv)
    dwout_s[...] += dot_tn(o_ref[0], dy_low)

    @pl.when(step == steps - 1)
    def _():
        scale = float(length * steps * r_size * c_size) ** (-0.5)
        parity = lax.rem(lax.axis_index("cols"), 2)
        for i in range(3):
            grad = (dwqkv_s[:, i * d : (i + 1) * d] * scale).astype(BF)
            store_rows(keep_ref, send_ref, parity, i * d, grad)
        store_rows(keep_ref, send_ref, parity, 3 * d, (dwout_s[...] * scale).astype(BF))
        gains = jnp.concatenate(
            [dg_s[...], dgc_ref[...], dgm_ref[...], jnp.zeros((5, d), F32)], axis=0
        )
        store_rows(keep_ref, send_ref, parity, 4 * d, (gains * scale).astype(BF))


def pack_tokens_kernel(dims, x_ref, b_ref, out_ref):
    r_size, c_size, wl, cpd, length, d = dims
    cells = x_ref.shape[1]
    rpd = cells // wl
    extra = out_ref.shape[1] - cells
    lane = lax.broadcasted_iota(jnp.int32, (wl, length), 1)
    cell = lax.broadcasted_iota(jnp.int32, (wl, length), 0)
    place = (lane == cell + lax.axis_index("cols") * wl).astype(F32).astype(BF)
    spread = dot(b_ref[...], place)
    parts = length // d
    for s in range(c_size):
        out_ref[s, :cells] = x_ref[s]
        rows = [
            spread[s * rpd + i : s * rpd + i + 1, t * d : (t + 1) * d]
            for i in range(rpd)
            for t in range(parts)
        ]
        if extra > rpd * parts:
            rows.append(jnp.zeros((extra - rpd * parts, d), F32))
        out_ref[s, cells:] = jnp.concatenate(rows, axis=0).astype(BF)


def pack_cotangent_kernel(dims, ct_ref, b_ref, *out_refs):
    r_size, hl, cpd, length, d = dims
    r_at = lax.axis_index("rows")
    lane = lax.broadcasted_iota(jnp.int32, (hl, d), 1)
    cell = lax.broadcasted_iota(jnp.int32, (hl, d), 0)
    place = (lane == cell + r_at * hl).astype(F32).astype(BF)
    spread = dot_tn(b_ref[...], place)
    for s in range(r_size):
        for r in range(r_size):

            @pl.when(jnp.bitwise_xor(r_at, s) == r)
            def _():
                out_refs[s][: hl * cpd] = (
                    ct_ref[:, r * cpd : (r + 1) * cpd, :].astype(F32).reshape(hl * cpd, d).astype(BF)
                )
                rows = spread[r * cpd : (r + 1) * cpd]
                if cpd % 8:
                    rows = jnp.concatenate([rows, jnp.zeros((-cpd % 8, d), F32)], axis=0)
                out_refs[s][hl * cpd :] = rows.astype(BF)


def weight_grad_kernel(
    scale, h2_ref, dqkv_ref, o2_ref, dy2_ref, h3_ref, du_ref, act_ref, ct_ref,
    keep_ref, send_ref, dwqkv_s, dwout_s, dwup_s, dwdown_s,
):
    step, steps = pl.program_id(0), pl.num_programs(0)
    sums = (
        (dwqkv_s, h2_ref, dqkv_ref),
        (dwout_s, o2_ref, dy2_ref),
        (dwup_s, h3_ref, du_ref),
        (dwdown_s, act_ref, ct_ref),
    )

    @pl.when(step == 0)
    def _():
        for total, left, right in sums:
            total[...] = dot_tn(left[...], right[...])

    @pl.when(step != 0)
    def _():
        for total, left, right in sums:
            total[...] += dot_tn(left[...], right[...])

    @pl.when(step == steps - 1)
    def _():
        parity = lax.rem(lax.axis_index("cols"), 2)
        d = dwout_s.shape[0]
        row = 0
        for total, _, _ in sums[:3]:
            for i in range(total.shape[1] // d):
                grad = (total[:, i * d : (i + 1) * d] * scale).astype(BF)
                store_rows(keep_ref, send_ref, parity, row, grad)
                row += d
        store_rows(keep_ref, send_ref, parity, row, (dwdown_s[...] * scale).astype(BF))
        row += dwdown_s.shape[0]
        if row < 2 * keep_ref.shape[0]:
            rest = jnp.zeros((2 * keep_ref.shape[0] - row, d), BF)
            store_rows(keep_ref, send_ref, parity, row, rest)


def unpack_kernel(dims, own_ref, got_ref, *out_refs):
    r_size, z_size, col_rows, row_rows, d, layout = dims
    r_at, c_at = lax.axis_index("rows"), lax.axis_index("cols")
    z_at, parity = lax.div(c_at, 2), lax.rem(c_at, 2)
    for core in range(2):
        for r in range(r_size):
            for z in range(z_size):
                at = (core * r_size + r) * z_size + z
                s, t = jnp.bitwise_xor(r_at, r), jnp.bitwise_xor(z_at, z)
                for base, size, sections in (
                    (0, col_rows, layout[0]),
                    (col_rows, row_rows, layout[1]),
                ):
                    first = at * size
                    for start, stop, which, row0, lane0 in sections:
                        low, high = max(first, start), min(first + size, stop)
                        if low >= high:
                            continue
                        cut = slice(base + low - first, base + high - first)
                        to = slice(row0 + low - start, row0 + high - start)
                        lanes = slice(lane0, lane0 + d)
                        out_ref = out_refs[which]

                        @pl.when(parity == core)
                        def _():
                            out_ref[to, lanes] = own_ref[s, t, cut, :].astype(F32)

                        @pl.when(parity != core)
                        def _():
                            out_ref[to, lanes] = got_ref[s, t, cut, :].astype(F32)


def column_kernel(
    dims, *refs
):
    r_size, hl, cpd, length, d, chunk = dims
    y_ref, *ct_refs = refs[: 1 + r_size]
    (
        gain_ref, wqkv_ref, wout_ref, gmlp_ref, wup_ref, wdown_ref,
        dy_ref, h2_ref, dqkv_ref, o2_ref, dy2_ref, h3_ref, du_ref, act_ref, ctc_ref,
        dg_ref, dgm_ref, wire_s, x_s, ct_s, bias_s, p_s,
    ) = refs[1 + r_size :]
    step, steps = pl.program_id(0), pl.num_programs(0)
    factor = float(d // HEADS) ** (-0.5)
    masks = head_masks(d)
    tokens = chunk * length

    r_at = lax.axis_index("rows")

    @pl.when(step == 0)
    def _():
        for lanes in range(d // LANES):
            cut = slice(lanes * LANES, (lanes + 1) * LANES)
            wire_s[lanes] = y_ref[:, cut].astype(F32)
            for j in range(cpd):
                x_s[j, :, cut] = wire_s[lanes, pl.ds(j, length, stride=cpd), :]
        block = hl * cpd
        for lanes in range(d // LANES):
            cut = slice(lanes * LANES, (lanes + 1) * LANES)
            for s in range(r_size):
                source = jnp.bitwise_xor(r_at, s)
                to = pl.ds(pl.multiple_of(source * block, block), block)
                wire_s[lanes, to, :] = ct_refs[s][:block, cut].astype(F32)
            for j in range(cpd):
                ct_s[j, :, cut] = wire_s[lanes, pl.ds(j, length, stride=cpd), :]
        total = ct_refs[0][block:].astype(F32)
        for s in range(1, r_size):
            total = total + ct_refs[s][block:].astype(F32)
        for j in range(cpd):
            bias_s[j] = total[j : j + 1, :length]
        dg_ref[...] = jnp.zeros_like(dg_ref)
        dgm_ref[...] = jnp.zeros_like(dgm_ref)

    at = pl.ds(step * chunk, chunk)
    x = x_s[at].reshape(tokens, d)
    ct = ct_s[at].reshape(tokens, d)
    n2, r2 = norm(x)
    h2 = (n2 * gain_ref[...]).astype(BF)
    h2_ref[...] = h2
    qkv = dot(h2, wqkv_ref[...]).astype(BF)
    outs = []
    for j in range(chunk):
        part = slice(j * length, (j + 1) * length)
        q, k, v = qkv[part, :d], qkv[part, d : 2 * d], qkv[part, 2 * d :]
        weights = softmax_heads(q, k, bias_s[step * chunk + j], masks, factor)
        for i in range(HEADS):
            p_s[j, i] = weights[i]
        outs.append(mix_heads([w.astype(BF) for w in weights], v, masks))
    o2 = jnp.concatenate(outs, axis=0).astype(BF)
    o2_ref[...] = o2
    y2 = (x + dot(o2, wout_ref[...])).astype(BF).astype(F32)
    n3, r3 = norm(y2)
    h3 = (n3 * gmlp_ref[...]).astype(BF)
    h3_ref[...] = h3
    ct_low = ct.astype(BF)
    ctc_ref[...] = ct_low
    u = dot(h3, wup_ref[...])
    root = 0.7978845608028654
    square = u * u
    t = jnp.tanh(root * (u + 0.044715 * (u * square)))
    act_ref[...] = (0.5 * u * (1.0 + t)).astype(BF)
    slope = 0.5 * (1.0 + t) + 0.5 * u * (1.0 - t * t) * (root * (1.0 + 3.0 * 0.044715 * square))
    du = (dot_nt(ct_low, wdown_ref[...]) * slope).astype(BF)
    du_ref[...] = du
    g3 = dot_nt(du, wup_ref[...])
    dgm_ref[...] += jnp.sum(g3 * n3, axis=0, keepdims=True)
    dy2 = (ct + norm_back(g3, n3, r3, gmlp_ref[...])).astype(BF)
    dy2_ref[...] = dy2
    do = dot_nt(dy2, wout_ref[...]).astype(BF)
    grads = []
    for j in range(chunk):
        part = slice(j * length, (j + 1) * length)
        q, k, v = qkv[part, :d], qkv[part, d : 2 * d], qkv[part, 2 * d :]
        weights = [p_s[j, i] for i in range(HEADS)]
        low = [w.astype(BF) for w in weights]
        grads.append(
            jnp.concatenate(heads_back(weights, low, do[part], q, k, v, masks, factor), axis=1)
        )
    dqkv = jnp.concatenate(grads, axis=0)
    dqkv_ref[...] = dqkv
    g2 = dot_nt(dqkv, wqkv_ref[...])
    dg_ref[...] += jnp.sum(g2 * n2, axis=0, keepdims=True)
    dy1 = dy2.astype(F32) + norm_back(g2, n2, r2, gain_ref[...])
    x_s[at] = dy1.reshape(chunk, length, d)

    @pl.when(step == steps - 1)
    def _():
        for lanes in range(d // LANES):
            cut = slice(lanes * LANES, (lanes + 1) * LANES)
            for j in range(cpd):
                wire_s[lanes, pl.ds(j, length, stride=cpd), :] = x_s[j, :, cut]
            dy_ref[:, cut] = wire_s[lanes].astype(BF)


def whole(shape):
    return pl.BlockSpec(shape, lambda i: (0,) * len(shape))


def params():
    return pltpu.CompilerParams(
        dimension_semantics=("arbitrary",), vmem_limit_bytes=VMEM_LIMIT
    )


def whole(shape):
    return pl.BlockSpec(shape, lambda i: (0,) * len(shape))


def params():
    return pltpu.CompilerParams(
        dimension_semantics=("arbitrary",), vmem_limit_bytes=VMEM_LIMIT
    )


def row_forward(dims, rpd, recv, gain, w_qkv, w_out):
    r_size, c_size, wl, cpd, length, d = dims
    n_dev = r_size * c_size
    extra = recv.shape[1] - rpd * wl
    return pl.pallas_call(
        functools.partial(row_forward_kernel, dims),
        grid=(rpd,),
        in_specs=[
            pl.BlockSpec((c_size, wl, d), lambda i: (0, i, 0)),
            pl.BlockSpec((c_size, extra, d), lambda i: (0, rpd * wl // extra, 0)),
            whole((1, d)),
            whole((d, 3 * d)),
            whole((d, d)),
        ],
        out_specs=[
            pl.BlockSpec((n_dev, 1, cpd, d), lambda i: (0, i, 0, 0)),
            pl.BlockSpec((1, length, 3 * d), lambda i: (i, 0, 0)),
            pl.BlockSpec((1, length, d), lambda i: (i, 0, 0)),
            pl.BlockSpec((1, HEADS, length, length), lambda i: (i, 0, 0, 0)),
        ],
        out_shape=[
            jax.ShapeDtypeStruct((n_dev, rpd, cpd, d), BF),
            jax.ShapeDtypeStruct((rpd, length, 3 * d), BF),
            jax.ShapeDtypeStruct((rpd, length, d), BF),
            jax.ShapeDtypeStruct((rpd, HEADS, length, length), BF),
        ],
        compiler_params=params(),
        name="row_forward",
    )(recv, recv, gain, w_qkv, w_out)


def row_backward(dims, rpd, half, recv, dy, qkv, o, p, gain, w_qkv, w_out, dg_col, dg_mlp):
    r_size, c_size, wl, cpd, length, d = dims
    n_dev = r_size * c_size
    return pl.pallas_call(
        functools.partial(row_backward_kernel, dims),
        grid=(rpd,),
        in_specs=[
            pl.BlockSpec((c_size, wl, d), lambda i: (0, i, 0)),
            pl.BlockSpec((n_dev, 1, cpd, d), lambda i: (0, i, 0, 0)),
            pl.BlockSpec((1, length, 3 * d), lambda i: (i, 0, 0)),
            pl.BlockSpec((1, length, d), lambda i: (i, 0, 0)),
            pl.BlockSpec((1, HEADS, length, length), lambda i: (i, 0, 0, 0)),
            whole((1, d)),
            whole((d, 3 * d)),
            whole((d, d)),
            whole((1, d)),
            whole((1, d)),
        ],
        out_specs=[
            pl.BlockSpec((c_size, wl, d), lambda i: (0, i, 0)),
            whole((half, d)),
            whole((half, d)),
        ],
        out_shape=[
            jax.ShapeDtypeStruct((c_size, rpd * wl, d), BF),
            jax.ShapeDtypeStruct((half, d), BF),
            jax.ShapeDtypeStruct((half, d), BF),
        ],
        scratch_shapes=[
            pltpu.VMEM((1, d), F32),
            pltpu.VMEM((d, 3 * d), F32),
            pltpu.VMEM((d, d), F32),
        ],
        compiler_params=params(),
        name="row_backward",
    )(recv, dy, qkv, o, p, gain, w_qkv, w_out, dg_col, dg_mlp)


def column_stage(dims, y_wire, ct_blocks, gain, w_qkv, w_out, gain_mlp, w_up, w_down):
    r_size, hl, cpd, length, d, chunk = dims
    tokens = cpd * length
    ff = w_up.shape[1]
    part = chunk * length

    def rows_of(width):
        return pl.BlockSpec((part, width), lambda i: (i, 0))

    def shape_of(width):
        return jax.ShapeDtypeStruct((tokens, width), BF)

    widths = (d, 3 * d, d, d, d, ff, ff, d)
    return pl.pallas_call(
        functools.partial(column_kernel, dims),
        grid=(cpd // chunk,),
        in_specs=[
            whole((tokens, d)),
            *[whole(block.shape) for block in ct_blocks],
            whole((1, d)),
            whole((d, 3 * d)),
            whole((d, d)),
            whole((1, d)),
            whole((d, ff)),
            whole((ff, d)),
        ],
        out_specs=[whole((tokens, d))] + [rows_of(w) for w in widths] + [whole((1, d))] * 2,
        out_shape=[shape_of(d)]
        + [shape_of(w) for w in widths]
        + [jax.ShapeDtypeStruct((1, d), F32)] * 2,
        scratch_shapes=[
            pltpu.VMEM((d // LANES, tokens, LANES), F32),
            pltpu.VMEM((cpd, length, d), F32),
            pltpu.VMEM((cpd, length, d), F32),
            pltpu.VMEM((cpd, 1, length), F32),
            pltpu.VMEM((chunk, HEADS, length, length), F32),
        ],
        compiler_params=params(),
        name="column_stage",
    )(y_wire, *ct_blocks, gain, w_qkv, w_out, gain_mlp, w_up, w_down)


def pack_tokens(dims, extra, tokens, key_bias):
    c_size, cells, d = tokens.shape
    return pl.pallas_call(
        functools.partial(pack_tokens_kernel, dims),
        out_shape=jax.ShapeDtypeStruct((c_size, cells + extra, d), BF),
        compiler_params=pltpu.CompilerParams(vmem_limit_bytes=VMEM_LIMIT),
        name="pack_tokens",
    )(tokens, key_bias)


def pack_cotangent(dims, cotangent, key_bias):
    r_size, hl, cpd, length, d = dims
    rows = hl * cpd + cpd + -cpd % 8
    return pl.pallas_call(
        functools.partial(pack_cotangent_kernel, dims),
        out_shape=[jax.ShapeDtypeStruct((rows, d), BF)] * r_size,
        compiler_params=pltpu.CompilerParams(vmem_limit_bytes=VMEM_LIMIT),
        name="pack_cotangent",
    )(cotangent, key_bias)


def weight_grads(scale, half, steps, pairs):
    d = pairs[1][0].shape[1]
    flat = [x for pair in pairs for x in pair]
    part = flat[0].shape[0] // steps
    return pl.pallas_call(
        functools.partial(weight_grad_kernel, scale),
        grid=(steps,),
        in_specs=[pl.BlockSpec((part, x.shape[1]), lambda i: (i, 0)) for x in flat],
        out_specs=[whole((half, d))] * 2,
        out_shape=[jax.ShapeDtypeStruct((half, d), BF)] * 2,
        scratch_shapes=[pltpu.VMEM((left.shape[1], right.shape[1]), F32) for left, right in pairs],
        compiler_params=params(),
        name="weight_grads",
    )(*flat)


def unpack(dims, own, got, shapes):
    return pl.pallas_call(
        functools.partial(unpack_kernel, dims),
        out_shape=[jax.ShapeDtypeStruct(shape, F32) for shape in shapes],
        compiler_params=pltpu.CompilerParams(vmem_limit_bytes=VMEM_LIMIT),
        name="unpack",
    )(own, got)


def exchange(x, axes):
    return lax.all_to_all(x, axes, split_axis=0, concat_axis=0, tiled=True)


def swap(x, axis, step):
    size = lax.axis_size(axis)
    return lax.ppermute(x, axis, [(i, i ^ step) for i in range(size)])


def add(parts):
    total = parts[0].astype(F32)
    for part in parts[1:]:
        total = total + part.astype(F32)
    return total.astype(BF)


def scatter_sum(blocks, axis, at, unit):
    n = blocks.shape[0]
    parts = [lax.dynamic_index_in_dim(blocks, at, 0, keepdims=False)]
    for s in range(1, n):
        block = lax.dynamic_index_in_dim(blocks, jnp.bitwise_xor(at, s), 0, keepdims=False)
        parts.append(swap(block, axis, s * unit))
    return add(parts)


def gather(block, axis, n, unit):
    return jnp.stack([block] + [swap(block, axis, s * unit) for s in range(1, n)])


def padded(rows, unit):
    return rows + -rows % unit


def shards(
    tokens, key_bias, cotangent, gain_row, w_qkv_row, w_out_row,
    gain_col, w_qkv_col, w_out_col, gain_mlp, w_up, w_down,
):
    r_size, c_size = lax.axis_size("rows"), lax.axis_size("cols")
    hl, wl, d = tokens.shape
    ff = w_up.shape[1]
    rpd, cpd = hl // c_size, wl // r_size
    row_len, col_len = wl * c_size, hl * r_size
    scale = float(row_len * col_len) ** (-0.5)
    r_at, c_at = lax.axis_index("rows"), lax.axis_index("cols")
    z_size, z_at = c_size // 2, lax.axis_index("cols") // 2
    row_dims = (r_size, c_size, wl, cpd, row_len, d)
    chunk = min(cpd, max(1, 512 // col_len))
    col_dims = (r_size, hl, cpd, col_len, d, chunk)
    unit = 8 * 2 * r_size * z_size
    col_half = padded(3 * d + d + 2 * ff, unit) // 2
    row_half = padded(4 * d + 8, unit) // 2

    extra = padded(rpd * row_len // d, 8)
    recv = exchange(
        pack_tokens(row_dims, extra, tokens.reshape(c_size, rpd * wl, d), key_bias), "cols"
    )
    ct_blocks = pack_cotangent(col_dims[:5], cotangent, key_bias)
    ct_blocks = [ct_blocks[0]] + [swap(ct_blocks[s], "rows", s) for s in range(1, r_size)]

    y_send, qkv1, o1, p1 = row_forward(row_dims, rpd, recv, gain_row[None], w_qkv_row, w_out_row)
    y_wire = exchange(y_send, ALL).reshape(hl * r_size * cpd, d)
    (dy_send, h2, dqkv2, o2, dy2, h3, du, act, ct_cols, dg_col, dg_mlp) = column_stage(
        col_dims, y_wire, ct_blocks, gain_col[None], w_qkv_col, w_out_col,
        gain_mlp[None], w_up, w_down,
    )
    dy_wire = exchange(dy_send.reshape(y_send.shape), ALL)

    keep, send = weight_grads(
        scale, col_half, 4, ((h2, dqkv2), (o2, dy2), (h3, du), (act, ct_cols))
    )
    col_sum = add([keep, swap(send, "cols", 1)])
    col_sum = scatter_sum(col_sum.reshape(r_size, -1, d), "rows", r_at, 1)

    dt_send, keep, send = row_backward(
        row_dims, rpd, row_half, recv, dy_wire, qkv1, o1, p1, gain_row[None], w_qkv_row,
        w_out_row, dg_col, dg_mlp,
    )
    d_tokens = exchange(dt_send, "cols").reshape(hl, wl, d)
    row_sum = add([keep, swap(send, "cols", 1)])
    row_sum = scatter_sum(row_sum.reshape(r_size, -1, d), "rows", r_at, 1)
    both = jnp.concatenate(
        [col_sum.reshape(z_size, -1, d), row_sum.reshape(z_size, -1, d)], axis=1
    )
    both = scatter_sum(both, "cols", z_at, 2)
    both = gather(both, "cols", z_size, 2)
    both = gather(both, "rows", r_size, 1)
    other = swap(both, "cols", 1)

    nff = ff // d
    col_layout = [(i * d, (i + 1) * d, 4, 0, i * d) for i in range(3)]
    col_layout += [(3 * d, 4 * d, 5, 0, 0)]
    col_layout += [((4 + i) * d, (5 + i) * d, 7, 0, i * d) for i in range(nff)]
    col_layout += [((4 + nff) * d, (4 + nff) * d + ff, 8, 0, 0)]
    row_layout = [(i * d, (i + 1) * d, 1, 0, i * d) for i in range(3)]
    row_layout += [(3 * d, 4 * d, 2, 0, 0), (4 * d, 4 * d + 8, 0, 0, 0)]
    shapes = [
        (8, d), (d, 3 * d), (d, d), (8, d), (d, 3 * d), (d, d), (8, d), (d, ff), (ff, d),
    ]
    shapes = [s for i, s in enumerate(shapes) if i not in (3, 6)]
    index = {0: 0, 1: 1, 2: 2, 4: 3, 5: 4, 7: 5, 8: 6}
    layout = tuple(
        tuple((a, b, index[w], r, l) for a, b, w, r, l in part)
        for part in (col_layout, row_layout)
    )
    dims = (r_size, z_size, 2 * col_half // (2 * r_size * z_size),
            2 * row_half // (2 * r_size * z_size), d, layout)
    gains, qkv_row, out_row, qkv_col, out_col, up, down = unpack(dims, both, other, shapes)
    return (
        d_tokens, gains[0], qkv_row, out_row, gains[1], qkv_col, out_col, gains[2], up, down,
    )


def solution(mesh):
    cells = P("rows", "cols", None)
    in_specs = (cells, P("rows", "cols"), cells) + (P(),) * 9
    out_specs = (cells,) + (P(),) * 9
    return jax.shard_map(shards, mesh=mesh, in_specs=in_specs, out_specs=out_specs, check_vma=False)
```

```python
import functools
import jax
import jax.numpy as jnp
from jax import lax
from jax.experimental import pallas as pl
from jax.experimental.pallas import tpu as pltpu
from jax.sharding import PartitionSpec as P

HEADS = 4
LANES = 128
ALL = ("rows", "cols")
BF = jnp.bfloat16
F32 = jnp.float32
VMEM_LIMIT = 56 * 1024 * 1024


def dot(a, b):
    return lax.dot_general(a, b, (((1,), (0,)), ((), ())), preferred_element_type=F32)


def dot_nt(a, b):
    return lax.dot_general(a, b, (((1,), (1,)), ((), ())), preferred_element_type=F32)


def dot_tn(a, b):
    return lax.dot_general(a, b, (((0,), (0,)), ((), ())), preferred_element_type=F32)


def norm(x):
    centred = x - jnp.mean(x, axis=-1, keepdims=True)
    inverse = lax.rsqrt(jnp.mean(centred * centred, axis=-1, keepdims=True) + 1e-05)
    return centred * inverse, inverse


def norm_back(grad, normed, inverse, gain):
    scaled = grad * gain
    return inverse * (
        scaled
        - jnp.mean(scaled, axis=-1, keepdims=True)
        - normed * jnp.mean(scaled * normed, axis=-1, keepdims=True)
    )


def head_masks(features):
    lane = lax.broadcasted_iota(jnp.int32, (1, features), 1) // (features // HEADS)
    return [(lane == h).astype(F32).astype(BF) for h in range(HEADS)]


def softmax_heads(q, k, bias, masks, factor):
    weights = []
    for mask in masks:
        s = dot_nt(q * (mask * factor), k) + bias
        e = jnp.exp(s - jnp.max(s, axis=-1, keepdims=True))
        weights.append(e * (1.0 / jnp.sum(e, axis=-1, keepdims=True)))
    return weights


def mix_heads(weights_low, v, masks):
    return dot(
        jnp.concatenate(weights_low, axis=1),
        jnp.concatenate([v * mask for mask in masks], axis=0),
    )


def heads_back(weights, weights_low, do, q, k, v, masks, factor):
    dos = [do * mask for mask in masks]
    low = []
    for h in range(HEADS):
        dp = dot_nt(dos[h], v)
        p = weights[h]
        centre = jnp.sum(p * dp, axis=-1, keepdims=True)
        low.append((p * (dp - centre) * factor).astype(BF))
    dq = dot(
        jnp.concatenate(low, axis=1), jnp.concatenate([k * mask for mask in masks], axis=0)
    )
    dk = dot_tn(
        jnp.concatenate(low, axis=0), jnp.concatenate([q * mask for mask in masks], axis=0)
    )
    dv = dot_tn(jnp.concatenate(weights_low, axis=0), jnp.concatenate(dos, axis=0))
    return dq.astype(BF), dk.astype(BF), dv.astype(BF)


def load_cells(ref, pieces):
    return jnp.concatenate([ref[s].astype(F32) for s in range(pieces)], axis=0)


def row_bias(b_ref, row, pieces, length):
    total = b_ref[0].astype(F32)
    for s in range(1, pieces):
        total = total + b_ref[s].astype(F32)
    features = total.shape[1]
    at = lax.broadcasted_iota(jnp.int32, total.shape, 0)
    parts = length // features
    return jnp.concatenate(
        [
            jnp.sum(jnp.where(at == row * parts + t, total, 0.0), axis=0, keepdims=True)
            for t in range(parts)
        ],
        axis=1,
    )


def row_forward_kernel(
    dims, x_ref, b_ref, gain_ref, wqkv_ref, wout_ref, y_ref, qkv_ref, o_ref, p_ref
):
    r_size, c_size, wl, cpd, length, d = dims
    factor = float(d // HEADS) ** (-0.5)
    masks = head_masks(d)
    x = load_cells(x_ref, c_size)
    n, _ = norm(x)
    h = (n * gain_ref[...]).astype(BF)
    qkv = dot(h, wqkv_ref[...]).astype(BF)
    qkv_ref[0] = qkv
    q, k, v = qkv[:, :d], qkv[:, d : 2 * d], qkv[:, 2 * d :]
    bias = row_bias(b_ref, pl.program_id(0), c_size, length)
    weights = softmax_heads(q, k, bias, masks, factor)
    low = [w.astype(BF) for w in weights]
    for i in range(HEADS):
        p_ref[0, i] = low[i]
    o = mix_heads(low, v, masks).astype(BF)
    o_ref[0] = o
    y = (x + dot(o, wout_ref[...])).astype(BF)
    for c in range(c_size):
        for r in range(r_size):
            at = c * wl + r * cpd
            y_ref[r * c_size + c, 0] = y[at : at + cpd]


def store_rows(keep_ref, send_ref, parity, row, value):
    half = keep_ref.shape[0]
    for side in range(2):
        start, stop = max(row, side * half), min(row + value.shape[0], (side + 1) * half)
        if start < stop:
            piece = value[start - row : stop - row]
            to = slice(start - side * half, stop - side * half)

            @pl.when(parity == side)
            def _():
                keep_ref[to] = piece

            @pl.when(parity != side)
            def _():
                send_ref[to] = piece


def row_backward_kernel(
    dims, x_ref, dy_ref, qkv_ref, o_ref, p_ref, gain_ref, wqkv_ref, wout_ref, dgc_ref, dgm_ref,
    dt_ref, keep_ref, send_ref, dg_s, dwqkv_s, dwout_s,
):
    r_size, c_size, wl, cpd, length, d = dims
    step, steps = pl.program_id(0), pl.num_programs(0)
    factor = float(d // HEADS) ** (-0.5)
    masks = head_masks(d)

    @pl.when(step == 0)
    def _():
        dg_s[...] = jnp.zeros_like(dg_s)
        dwqkv_s[...] = jnp.zeros_like(dwqkv_s)
        dwout_s[...] = jnp.zeros_like(dwout_s)
        keep_ref[...] = jnp.zeros_like(keep_ref)
        send_ref[...] = jnp.zeros_like(send_ref)

    dy = jnp.concatenate(
        [dy_ref[r * c_size + c, 0].astype(F32) for c in range(c_size) for r in range(r_size)],
        axis=0,
    )
    dy_low = dy.astype(BF)
    do = dot_nt(dy_low, wout_ref[...]).astype(BF)
    qkv = qkv_ref[0]
    q, k, v = qkv[:, :d], qkv[:, d : 2 * d], qkv[:, 2 * d :]
    low = [p_ref[0, i] for i in range(HEADS)]
    weights = [w.astype(F32) for w in low]
    dq, dk, dv = heads_back(weights, low, do, q, k, v, masks, factor)
    dqkv = jnp.concatenate([dq, dk, dv], axis=1)
    g = dot_nt(dqkv, wqkv_ref[...])
    n, inverse = norm(load_cells(x_ref, c_size))
    h = (n * gain_ref[...]).astype(BF)
    dt = (dy + norm_back(g, n, inverse, gain_ref[...])).astype(BF)
    for s in range(c_size):
        dt_ref[s] = dt[s * wl : (s + 1) * wl]
    dg_s[...] += jnp.sum(g * n, axis=0, keepdims=True)
    dwqkv_s[...] += dot_tn(h, dqkv)
    dwout_s[...] += dot_tn(o_ref[0], dy_low)

    @pl.when(step == steps - 1)
    def _():
        scale = float(length * steps * r_size * c_size) ** (-0.5)
        parity = lax.rem(lax.axis_index("cols"), 2)
        for i in range(3):
            grad = (dwqkv_s[:, i * d : (i + 1) * d] * scale).astype(BF)
            store_rows(keep_ref, send_ref, parity, i * d, grad)
        store_rows(keep_ref, send_ref, parity, 3 * d, (dwout_s[...] * scale).astype(BF))
        gains = jnp.concatenate(
            [dg_s[...], dgc_ref[...], dgm_ref[...], jnp.zeros((5, d), F32)], axis=0
        )
        store_rows(keep_ref, send_ref, parity, 4 * d, (gains * scale).astype(BF))


def pack_tokens_kernel(dims, x_ref, b_ref, out_ref):
    r_size, c_size, wl, cpd, length, d = dims
    cells = x_ref.shape[1]
    rpd = cells // wl
    extra = out_ref.shape[1] - cells
    lane = lax.broadcasted_iota(jnp.int32, (wl, length), 1)
    cell = lax.broadcasted_iota(jnp.int32, (wl, length), 0)
    place = (lane == cell + lax.axis_index("cols") * wl).astype(F32).astype(BF)
    spread = dot(b_ref[...], place)
    parts = length // d
    for s in range(c_size):
        out_ref[s, :cells] = x_ref[s]
        rows = [
            spread[s * rpd + i : s * rpd + i + 1, t * d : (t + 1) * d]
            for i in range(rpd)
            for t in range(parts)
        ]
        if extra > rpd * parts:
            rows.append(jnp.zeros((extra - rpd * parts, d), F32))
        out_ref[s, cells:] = jnp.concatenate(rows, axis=0).astype(BF)


def pack_cotangent_kernel(dims, ct_ref, b_ref, *out_refs):
    r_size, hl, cpd, length, d = dims
    r_at = lax.axis_index("rows")
    lane = lax.broadcasted_iota(jnp.int32, (hl, d), 1)
    cell = lax.broadcasted_iota(jnp.int32, (hl, d), 0)
    place = (lane == cell + r_at * hl).astype(F32).astype(BF)
    spread = dot_tn(b_ref[...], place)
    for s in range(r_size):
        for r in range(r_size):

            @pl.when(jnp.bitwise_xor(r_at, s) == r)
            def _():
                out_refs[s][: hl * cpd] = (
                    ct_ref[:, r * cpd : (r + 1) * cpd, :].astype(F32).reshape(hl * cpd, d).astype(BF)
                )
                rows = spread[r * cpd : (r + 1) * cpd]
                if cpd % 8:
                    rows = jnp.concatenate([rows, jnp.zeros((-cpd % 8, d), F32)], axis=0)
                out_refs[s][hl * cpd :] = rows.astype(BF)


def weight_grad_kernel(scale, n_out, *refs):
    ins, out_refs = refs[:8], refs[8 : 8 + n_out]
    sums = refs[8 + n_out :]
    step, steps = pl.program_id(0), pl.num_programs(0)
    pairs = tuple(zip(sums, ins[::2], ins[1::2]))

    @pl.when(step == 0)
    def _():
        for total, left, right in pairs:
            total[...] = dot_tn(left[...], right[...])

    @pl.when(step != 0)
    def _():
        for total, left, right in pairs:
            total[...] += dot_tn(left[...], right[...])

    @pl.when(step == steps - 1)
    def _():
        r_at = lax.axis_index("rows")
        d = sums[1].shape[0]
        block = out_refs[0].shape[0]
        sections = []
        for total in sums[:3]:
            sections += [(total, slice(0, d), slice(i, i + d)) for i in range(0, total.shape[1], d)]
        sections += [(sums[3], slice(i, i + d), slice(0, d)) for i in range(0, sums[3].shape[0], d)]
        for r in range(n_out):
            for s in range(n_out):

                @pl.when(jnp.bitwise_xor(r_at, s) == r)
                def _():
                    end = len(sections) * d
                    for at in range(0, block, d):
                        size = min(d, block - at)
                        row = r * block + at
                        while size > 0:
                            if row < end:
                                total, rows, lanes = sections[row // d]
                                skip = row % d
                                part = min(size, d - skip)
                                rows = slice(rows.start + skip, rows.start + skip + part)
                                piece = (total[rows, lanes] * scale).astype(BF)
                            else:
                                part = size
                                piece = jnp.zeros((part, d), BF)
                            to = row - r * block
                            out_refs[s][to : to + part] = piece
                            row, size = row + part, size - part


def unpack_kernel(dims, own_ref, got_ref, *out_refs):
    r_size, z_size, col_rows, row_rows, d, layout = dims
    r_at, c_at = lax.axis_index("rows"), lax.axis_index("cols")
    z_at, parity = lax.div(c_at, 2), lax.rem(c_at, 2)
    for core in range(2):
        copies = []
        for r in range(r_size):
            for z in range(z_size):
                for base, size, sections, at in (
                    (0, col_rows, layout[0], (r * 2 + core) * z_size + z),
                    (col_rows, row_rows, layout[1], (core * r_size + r) * z_size + z),
                ):
                    first = at * size
                    for start, stop, which, row0, lane0 in sections:
                        low, high = max(first, start), min(first + size, stop)
                        if low < high:
                            cut = slice(base + low - first, base + high - first)
                            to = slice(row0 + low - start, row0 + high - start)
                            copies.append((r, z, cut, which, to, slice(lane0, lane0 + d)))

        def place(source):
            for r, z, cut, which, to, lanes in copies:
                s, t = jnp.bitwise_xor(r_at, r), jnp.bitwise_xor(z_at, z)
                piece = source[s, t, cut, :].astype(F32)
                if which < 0:
                    for i in range(3):
                        out_refs[i][...] = piece[i : i + 1]
                else:
                    out_refs[which][to, lanes] = piece

        @pl.when(parity == core)
        def _():
            place(own_ref)

        @pl.when(parity != core)
        def _():
            place(got_ref)


def column_kernel(
    dims, *refs
):
    r_size, hl, cpd, length, d, chunk = dims
    y_ref, *ct_refs = refs[: 1 + r_size]
    (
        gain_ref, wqkv_ref, wout_ref, gmlp_ref, wup_ref, wdown_ref,
        dy_ref, h2_ref, dqkv_ref, o2_ref, dy2_ref, h3_ref, du_ref, act_ref, ctc_ref,
        dg_ref, dgm_ref, wire_s, x_s, ct_s, bias_s, p_s,
    ) = refs[1 + r_size :]
    step, steps = pl.program_id(0), pl.num_programs(0)
    factor = float(d // HEADS) ** (-0.5)
    masks = head_masks(d)
    tokens = chunk * length

    r_at = lax.axis_index("rows")

    @pl.when(step == 0)
    def _():
        for lanes in range(d // LANES):
            cut = slice(lanes * LANES, (lanes + 1) * LANES)
            wire_s[lanes] = y_ref[:, cut].astype(F32)
            for j in range(cpd):
                x_s[j, :, cut] = wire_s[lanes, pl.ds(j, length, stride=cpd), :]
        block = hl * cpd
        for lanes in range(d // LANES):
            cut = slice(lanes * LANES, (lanes + 1) * LANES)
            for s in range(r_size):
                source = jnp.bitwise_xor(r_at, s)
                to = pl.ds(pl.multiple_of(source * block, block), block)
                wire_s[lanes, to, :] = ct_refs[s][:block, cut].astype(F32)
            for j in range(cpd):
                ct_s[j, :, cut] = wire_s[lanes, pl.ds(j, length, stride=cpd), :]
        total = ct_refs[0][block:].astype(F32)
        for s in range(1, r_size):
            total = total + ct_refs[s][block:].astype(F32)
        for j in range(cpd):
            bias_s[j] = total[j : j + 1, :length]
        dg_ref[...] = jnp.zeros_like(dg_ref)
        dgm_ref[...] = jnp.zeros_like(dgm_ref)

    at = pl.ds(step * chunk, chunk)
    x = x_s[at].reshape(tokens, d)
    ct = ct_s[at].reshape(tokens, d)
    n2, r2 = norm(x)
    h2 = (n2 * gain_ref[...]).astype(BF)
    h2_ref[...] = h2
    qkv = dot(h2, wqkv_ref[...]).astype(BF)
    outs = []
    for j in range(chunk):
        part = slice(j * length, (j + 1) * length)
        q, k, v = qkv[part, :d], qkv[part, d : 2 * d], qkv[part, 2 * d :]
        weights = softmax_heads(q, k, bias_s[step * chunk + j], masks, factor)
        for i in range(HEADS):
            p_s[j, i] = weights[i]
        outs.append(mix_heads([w.astype(BF) for w in weights], v, masks))
    o2 = jnp.concatenate(outs, axis=0).astype(BF)
    o2_ref[...] = o2
    y2 = (x + dot(o2, wout_ref[...])).astype(BF).astype(F32)
    n3, r3 = norm(y2)
    h3 = (n3 * gmlp_ref[...]).astype(BF)
    h3_ref[...] = h3
    ct_low = ct.astype(BF)
    ctc_ref[...] = ct_low
    u = dot(h3, wup_ref[...])
    root = 0.7978845608028654
    square = u * u
    t = jnp.tanh(root * (u + 0.044715 * (u * square)))
    act_ref[...] = (0.5 * u * (1.0 + t)).astype(BF)
    slope = 0.5 * (1.0 + t) + 0.5 * u * (1.0 - t * t) * (root * (1.0 + 3.0 * 0.044715 * square))
    du = (dot_nt(ct_low, wdown_ref[...]) * slope).astype(BF)
    du_ref[...] = du
    g3 = dot_nt(du, wup_ref[...])
    dgm_ref[...] += jnp.sum(g3 * n3, axis=0, keepdims=True)
    dy2 = (ct + norm_back(g3, n3, r3, gmlp_ref[...])).astype(BF)
    dy2_ref[...] = dy2
    do = dot_nt(dy2, wout_ref[...]).astype(BF)
    grads = []
    for j in range(chunk):
        part = slice(j * length, (j + 1) * length)
        q, k, v = qkv[part, :d], qkv[part, d : 2 * d], qkv[part, 2 * d :]
        weights = [p_s[j, i] for i in range(HEADS)]
        low = [w.astype(BF) for w in weights]
        grads.append(
            jnp.concatenate(heads_back(weights, low, do[part], q, k, v, masks, factor), axis=1)
        )
    dqkv = jnp.concatenate(grads, axis=0)
    dqkv_ref[...] = dqkv
    g2 = dot_nt(dqkv, wqkv_ref[...])
    dg_ref[...] += jnp.sum(g2 * n2, axis=0, keepdims=True)
    dy1 = dy2.astype(F32) + norm_back(g2, n2, r2, gain_ref[...])
    x_s[at] = dy1.reshape(chunk, length, d)

    @pl.when(step == steps - 1)
    def _():
        for lanes in range(d // LANES):
            cut = slice(lanes * LANES, (lanes + 1) * LANES)
            for j in range(cpd):
                wire_s[lanes, pl.ds(j, length, stride=cpd), :] = x_s[j, :, cut]
            dy_ref[:, cut] = wire_s[lanes].astype(BF)


def whole(shape):
    return pl.BlockSpec(shape, lambda i: (0,) * len(shape))


def params():
    return pltpu.CompilerParams(
        dimension_semantics=("arbitrary",), vmem_limit_bytes=VMEM_LIMIT
    )


def whole(shape):
    return pl.BlockSpec(shape, lambda i: (0,) * len(shape))


def params():
    return pltpu.CompilerParams(
        dimension_semantics=("arbitrary",), vmem_limit_bytes=VMEM_LIMIT
    )


def row_forward(dims, rpd, recv, gain, w_qkv, w_out):
    r_size, c_size, wl, cpd, length, d = dims
    n_dev = r_size * c_size
    extra = recv.shape[1] - rpd * wl
    return pl.pallas_call(
        functools.partial(row_forward_kernel, dims),
        grid=(rpd,),
        in_specs=[
            pl.BlockSpec((c_size, wl, d), lambda i: (0, i, 0)),
            pl.BlockSpec((c_size, extra, d), lambda i: (0, rpd * wl // extra, 0)),
            whole((1, d)),
            whole((d, 3 * d)),
            whole((d, d)),
        ],
        out_specs=[
            pl.BlockSpec((n_dev, 1, cpd, d), lambda i: (0, i, 0, 0)),
            pl.BlockSpec((1, length, 3 * d), lambda i: (i, 0, 0)),
            pl.BlockSpec((1, length, d), lambda i: (i, 0, 0)),
            pl.BlockSpec((1, HEADS, length, length), lambda i: (i, 0, 0, 0)),
        ],
        out_shape=[
            jax.ShapeDtypeStruct((n_dev, rpd, cpd, d), BF),
            jax.ShapeDtypeStruct((rpd, length, 3 * d), BF),
            jax.ShapeDtypeStruct((rpd, length, d), BF),
            jax.ShapeDtypeStruct((rpd, HEADS, length, length), BF),
        ],
        compiler_params=params(),
        name="row_forward",
    )(recv, recv, gain, w_qkv, w_out)


def row_backward(dims, rpd, half, recv, dy, qkv, o, p, gain, w_qkv, w_out, dg_col, dg_mlp):
    r_size, c_size, wl, cpd, length, d = dims
    n_dev = r_size * c_size
    return pl.pallas_call(
        functools.partial(row_backward_kernel, dims),
        grid=(rpd,),
        in_specs=[
            pl.BlockSpec((c_size, wl, d), lambda i: (0, i, 0)),
            pl.BlockSpec((n_dev, 1, cpd, d), lambda i: (0, i, 0, 0)),
            pl.BlockSpec((1, length, 3 * d), lambda i: (i, 0, 0)),
            pl.BlockSpec((1, length, d), lambda i: (i, 0, 0)),
            pl.BlockSpec((1, HEADS, length, length), lambda i: (i, 0, 0, 0)),
            whole((1, d)),
            whole((d, 3 * d)),
            whole((d, d)),
            whole((1, d)),
            whole((1, d)),
        ],
        out_specs=[
            pl.BlockSpec((c_size, wl, d), lambda i: (0, i, 0)),
            whole((half, d)),
            whole((half, d)),
        ],
        out_shape=[
            jax.ShapeDtypeStruct((c_size, rpd * wl, d), BF),
            jax.ShapeDtypeStruct((half, d), BF),
            jax.ShapeDtypeStruct((half, d), BF),
        ],
        scratch_shapes=[
            pltpu.VMEM((1, d), F32),
            pltpu.VMEM((d, 3 * d), F32),
            pltpu.VMEM((d, d), F32),
        ],
        compiler_params=params(),
        name="row_backward",
    )(recv, dy, qkv, o, p, gain, w_qkv, w_out, dg_col, dg_mlp)


def column_stage(dims, y_wire, ct_blocks, gain, w_qkv, w_out, gain_mlp, w_up, w_down):
    r_size, hl, cpd, length, d, chunk = dims
    tokens = cpd * length
    ff = w_up.shape[1]
    part = chunk * length

    def rows_of(width):
        return pl.BlockSpec((part, width), lambda i: (i, 0))

    def shape_of(width):
        return jax.ShapeDtypeStruct((tokens, width), BF)

    widths = (d, 3 * d, d, d, d, ff, ff, d)
    return pl.pallas_call(
        functools.partial(column_kernel, dims),
        grid=(cpd // chunk,),
        in_specs=[
            whole((tokens, d)),
            *[whole(block.shape) for block in ct_blocks],
            whole((1, d)),
            whole((d, 3 * d)),
            whole((d, d)),
            whole((1, d)),
            whole((d, ff)),
            whole((ff, d)),
        ],
        out_specs=[whole((tokens, d))] + [rows_of(w) for w in widths] + [whole((1, d))] * 2,
        out_shape=[shape_of(d)]
        + [shape_of(w) for w in widths]
        + [jax.ShapeDtypeStruct((1, d), F32)] * 2,
        scratch_shapes=[
            pltpu.VMEM((d // LANES, tokens, LANES), F32),
            pltpu.VMEM((cpd, length, d), F32),
            pltpu.VMEM((cpd, length, d), F32),
            pltpu.VMEM((cpd, 1, length), F32),
            pltpu.VMEM((chunk, HEADS, length, length), F32),
        ],
        compiler_params=params(),
        name="column_stage",
    )(y_wire, *ct_blocks, gain, w_qkv, w_out, gain_mlp, w_up, w_down)


def pack_tokens(dims, extra, tokens, key_bias):
    c_size, cells, d = tokens.shape
    return pl.pallas_call(
        functools.partial(pack_tokens_kernel, dims),
        out_shape=jax.ShapeDtypeStruct((c_size, cells + extra, d), BF),
        compiler_params=pltpu.CompilerParams(vmem_limit_bytes=VMEM_LIMIT),
        name="pack_tokens",
    )(tokens, key_bias)


def pack_cotangent(dims, cotangent, key_bias):
    r_size, hl, cpd, length, d = dims
    rows = hl * cpd + cpd + -cpd % 8
    return pl.pallas_call(
        functools.partial(pack_cotangent_kernel, dims),
        out_shape=[jax.ShapeDtypeStruct((rows, d), BF)] * r_size,
        compiler_params=pltpu.CompilerParams(vmem_limit_bytes=VMEM_LIMIT),
        name="pack_cotangent",
    )(cotangent, key_bias)


def weight_grads(scale, n_out, rows, steps, pairs):
    d = pairs[1][0].shape[1]
    flat = [x for pair in pairs for x in pair]
    part = flat[0].shape[0] // steps
    return pl.pallas_call(
        functools.partial(weight_grad_kernel, scale, n_out),
        grid=(steps,),
        in_specs=[pl.BlockSpec((part, x.shape[1]), lambda i: (i, 0)) for x in flat],
        out_specs=[whole((rows // n_out, d))] * n_out,
        out_shape=[jax.ShapeDtypeStruct((rows // n_out, d), BF)] * n_out,
        scratch_shapes=[pltpu.VMEM((left.shape[1], right.shape[1]), F32) for left, right in pairs],
        compiler_params=params(),
        name="weight_grads",
    )(*flat)


def unpack(dims, own, got, shapes):
    return pl.pallas_call(
        functools.partial(unpack_kernel, dims),
        out_shape=[jax.ShapeDtypeStruct(shape, F32) for shape in shapes],
        compiler_params=pltpu.CompilerParams(vmem_limit_bytes=VMEM_LIMIT),
        name="unpack",
    )(own, got)


def exchange(x, axes):
    return lax.all_to_all(x, axes, split_axis=0, concat_axis=0, tiled=True)


def swap(x, axis, step):
    size = lax.axis_size(axis)
    return lax.ppermute(x, axis, [(i, i ^ step) for i in range(size)])


def add(parts):
    total = parts[0].astype(F32)
    for part in parts[1:]:
        total = total + part.astype(F32)
    return total.astype(BF)


def scatter_sum(blocks, axis, at, unit):
    n = blocks.shape[0]
    parts = [lax.dynamic_index_in_dim(blocks, at, 0, keepdims=False)]
    for s in range(1, n):
        block = lax.dynamic_index_in_dim(blocks, jnp.bitwise_xor(at, s), 0, keepdims=False)
        parts.append(swap(block, axis, s * unit))
    return add(parts)


def gather(block, axis, n, unit):
    return jnp.stack([block] + [swap(block, axis, s * unit) for s in range(1, n)])


def padded(rows, unit):
    return rows + -rows % unit


def shards(
    tokens, key_bias, cotangent, gain_row, w_qkv_row, w_out_row,
    gain_col, w_qkv_col, w_out_col, gain_mlp, w_up, w_down,
):
    r_size, c_size = lax.axis_size("rows"), lax.axis_size("cols")
    hl, wl, d = tokens.shape
    ff = w_up.shape[1]
    rpd, cpd = hl // c_size, wl // r_size
    row_len, col_len = wl * c_size, hl * r_size
    scale = float(row_len * col_len) ** (-0.5)
    r_at, c_at = lax.axis_index("rows"), lax.axis_index("cols")
    z_size, z_at = c_size // 2, lax.axis_index("cols") // 2
    row_dims = (r_size, c_size, wl, cpd, row_len, d)
    chunk = min(cpd, max(1, 512 // col_len))
    col_dims = (r_size, hl, cpd, col_len, d, chunk)
    unit = 8 * 2 * r_size * z_size
    col_half = padded(3 * d + d + 2 * ff, unit) // 2
    row_half = padded(4 * d + 8, unit) // 2

    extra = padded(rpd * row_len // d, 8)
    recv = exchange(
        pack_tokens(row_dims, extra, tokens.reshape(c_size, rpd * wl, d), key_bias), "cols"
    )
    ct_blocks = pack_cotangent(col_dims[:5], cotangent, key_bias)
    ct_blocks = [ct_blocks[0]] + [swap(ct_blocks[s], "rows", s) for s in range(1, r_size)]

    y_send, qkv1, o1, p1 = row_forward(row_dims, rpd, recv, gain_row[None], w_qkv_row, w_out_row)
    y_wire = exchange(y_send, ALL).reshape(hl * r_size * cpd, d)
    (dy_send, h2, dqkv2, o2, dy2, h3, du, act, ct_cols, dg_col, dg_mlp) = column_stage(
        col_dims, y_wire, ct_blocks, gain_col[None], w_qkv_col, w_out_col,
        gain_mlp[None], w_up, w_down,
    )
    dy_wire = exchange(dy_send.reshape(y_send.shape), ALL)

    col_blocks = weight_grads(
        scale, r_size, 2 * col_half, 4, ((h2, dqkv2), (o2, dy2), (h3, du), (act, ct_cols))
    )
    col_sum = add(
        [col_blocks[0]] + [swap(col_blocks[s], "rows", s) for s in range(1, r_size)]
    )
    col_sum = scatter_sum(col_sum.reshape(2, -1, d), "cols", c_at % 2, 1)

    dt_send, keep, send = row_backward(
        row_dims, rpd, row_half, recv, dy_wire, qkv1, o1, p1, gain_row[None], w_qkv_row,
        w_out_row, dg_col, dg_mlp,
    )
    d_tokens = exchange(dt_send, "cols").reshape(hl, wl, d)
    row_sum = add([keep, swap(send, "cols", 1)])
    row_sum = scatter_sum(row_sum.reshape(r_size, -1, d), "rows", r_at, 1)
    both = jnp.concatenate(
        [col_sum.reshape(z_size, -1, d), row_sum.reshape(z_size, -1, d)], axis=1
    )
    both = scatter_sum(both, "cols", z_at, 2)
    both = gather(both, "cols", z_size, 2)
    both, d_tokens = lax.optimization_barrier((both, d_tokens))
    both = gather(both, "rows", r_size, 1)
    other = swap(both, "cols", 1)

    nff = ff // d
    col_layout = [(i * d, (i + 1) * d, 5, 0, i * d) for i in range(3)]
    col_layout += [(3 * d, 4 * d, 6, 0, 0)]
    col_layout += [((4 + i) * d, (5 + i) * d, 7, 0, i * d) for i in range(nff)]
    col_layout += [((4 + nff) * d, (4 + nff) * d + ff, 8, 0, 0)]
    row_layout = [(i * d, (i + 1) * d, 3, 0, i * d) for i in range(3)]
    row_layout += [(3 * d, 4 * d, 4, 0, 0), (4 * d, 4 * d + 8, -1, 0, 0)]
    layout = (tuple(col_layout), tuple(row_layout))
    shapes = [(1, d)] * 3 + [(d, 3 * d), (d, d), (d, 3 * d), (d, d), (d, ff), (ff, d)]
    dims = (r_size, z_size, 2 * col_half // (2 * r_size * z_size),
            2 * row_half // (2 * r_size * z_size), d, layout)
    outs = unpack(dims, both, other, shapes)
    g_row, g_col, g_mlp, qkv_row, out_row, qkv_col, out_col, up, down = outs
    return (
        d_tokens, g_row[0], qkv_row, out_row, g_col[0], qkv_col, out_col, g_mlp[0], up, down,
    )


def solution(mesh):
    cells = P("rows", "cols", None)
    in_specs = (cells, P("rows", "cols"), cells) + (P(),) * 9
    out_specs = (cells,) + (P(),) * 9
    return jax.shard_map(shards, mesh=mesh, in_specs=in_specs, out_specs=out_specs, check_vma=False)
```

```python
import functools
import jax
import jax.numpy as jnp
from jax import lax
from jax.experimental import pallas as pl
from jax.experimental.pallas import tpu as pltpu
from jax.sharding import PartitionSpec as P

HEADS = 4
LANES = 128
ALL = ("rows", "cols")
BF = jnp.bfloat16
F32 = jnp.float32
ROWS_FORWARD = 4
ROWS_BACKWARD = 2
VMEM_LIMIT = 56 * 1024 * 1024


def dot(a, b):
    return lax.dot_general(a, b, (((1,), (0,)), ((), ())), preferred_element_type=F32)


def dot_nt(a, b):
    return lax.dot_general(a, b, (((1,), (1,)), ((), ())), preferred_element_type=F32)


def dot_tn(a, b):
    return lax.dot_general(a, b, (((0,), (0,)), ((), ())), preferred_element_type=F32)


def norm(x):
    centred = x - jnp.mean(x, axis=-1, keepdims=True)
    inverse = lax.rsqrt(jnp.mean(centred * centred, axis=-1, keepdims=True) + 1e-05)
    return centred * inverse, inverse


def norm_back(grad, normed, inverse, gain):
    scaled = grad * gain
    return inverse * (
        scaled
        - jnp.mean(scaled, axis=-1, keepdims=True)
        - normed * jnp.mean(scaled * normed, axis=-1, keepdims=True)
    )


def head_masks(features):
    lane = lax.broadcasted_iota(jnp.int32, (1, features), 1) // (features // HEADS)
    return [(lane == h).astype(F32).astype(BF) for h in range(HEADS)]


def softmax_heads(q, k, bias, masks, factor):
    weights = []
    for mask in masks:
        s = dot_nt(q * (mask * factor), k) + bias
        e = jnp.exp(s - jnp.max(s, axis=-1, keepdims=True))
        weights.append(e * (1.0 / jnp.sum(e, axis=-1, keepdims=True)))
    return weights


def mix_heads(weights_low, v, masks):
    return dot(
        jnp.concatenate(weights_low, axis=1),
        jnp.concatenate([v * mask for mask in masks], axis=0),
    )


def heads_back(weights, weights_low, do, q, k, v, masks, factor):
    dos = [do * mask for mask in masks]
    low = []
    for h in range(HEADS):
        dp = dot_nt(dos[h], v)
        p = weights[h]
        centre = jnp.sum(p * dp, axis=-1, keepdims=True)
        low.append((p * (dp - centre) * factor).astype(BF))
    dq = dot(
        jnp.concatenate(low, axis=1), jnp.concatenate([k * mask for mask in masks], axis=0)
    )
    dk = dot_tn(
        jnp.concatenate(low, axis=0), jnp.concatenate([q * mask for mask in masks], axis=0)
    )
    dv = dot_tn(jnp.concatenate(weights_low, axis=0), jnp.concatenate(dos, axis=0))
    return dq.astype(BF), dk.astype(BF), dv.astype(BF)


def load_cells(ref, pieces, wl):
    rows = ref.shape[1] // wl
    return jnp.concatenate(
        [
            ref[s, i * wl : (i + 1) * wl].astype(F32)
            for i in range(rows)
            for s in range(pieces)
        ],
        axis=0,
    )


def row_bias(b_ref, row, pieces, length):
    total = b_ref[0].astype(F32)
    for s in range(1, pieces):
        total = total + b_ref[s].astype(F32)
    features = total.shape[1]
    at = lax.broadcasted_iota(jnp.int32, total.shape, 0)
    parts = length // features
    return jnp.concatenate(
        [
            jnp.sum(jnp.where(at == row * parts + t, total, 0.0), axis=0, keepdims=True)
            for t in range(parts)
        ],
        axis=1,
    )


def row_forward_kernel(
    dims, x_ref, b_ref, gain_ref, wqkv_ref, wout_ref, y_ref, qkv_ref, o_ref, p_ref
):
    r_size, c_size, wl, cpd, length, d = dims
    factor = float(d // HEADS) ** (-0.5)
    masks = head_masks(d)
    x = load_cells(x_ref, c_size, wl)
    rows = x_ref.shape[1] // wl
    n, _ = norm(x)
    h = (n * gain_ref[...]).astype(BF)
    qkv = dot(h, wqkv_ref[...]).astype(BF)
    outs = []
    for row in range(rows):
        part = slice(row * length, (row + 1) * length)
        qkv_ref[row] = qkv[part]
        q, k, v = qkv[part, :d], qkv[part, d : 2 * d], qkv[part, 2 * d :]
        bias = row_bias(b_ref, pl.program_id(0) * rows + row, c_size, length)
        low = [w.astype(BF) for w in softmax_heads(q, k, bias, masks, factor)]
        for i in range(HEADS):
            p_ref[row, i] = low[i]
        outs.append(mix_heads(low, v, masks).astype(BF))
        o_ref[row] = outs[row]
    y = (x + dot(jnp.concatenate(outs, axis=0), wout_ref[...])).astype(BF)
    for row in range(rows):
        for c in range(c_size):
            for r in range(r_size):
                at = row * length + c * wl + r * cpd
                y_ref[r * c_size + c, row] = y[at : at + cpd]


def store_rows(keep_ref, send_ref, parity, row, value):
    half = keep_ref.shape[0]
    for side in range(2):
        start, stop = max(row, side * half), min(row + value.shape[0], (side + 1) * half)
        if start < stop:
            piece = value[start - row : stop - row]
            to = slice(start - side * half, stop - side * half)

            @pl.when(parity == side)
            def _():
                keep_ref[to] = piece

            @pl.when(parity != side)
            def _():
                send_ref[to] = piece


def row_backward_kernel(
    dims, x_ref, dy_ref, qkv_ref, o_ref, p_ref, gain_ref, wqkv_ref, wout_ref, dgc_ref, dgm_ref,
    dt_ref, keep_ref, send_ref, dg_s, dwqkv_s, dwout_s,
):
    r_size, c_size, wl, cpd, length, d = dims
    step, steps = pl.program_id(0), pl.num_programs(0)
    factor = float(d // HEADS) ** (-0.5)
    masks = head_masks(d)

    @pl.when(step == 0)
    def _():
        dg_s[...] = jnp.zeros_like(dg_s)
        dwqkv_s[...] = jnp.zeros_like(dwqkv_s)
        dwout_s[...] = jnp.zeros_like(dwout_s)
        keep_ref[...] = jnp.zeros_like(keep_ref)
        send_ref[...] = jnp.zeros_like(send_ref)

    rows = dy_ref.shape[1]
    dy = jnp.concatenate(
        [
            dy_ref[r * c_size + c, row].astype(F32)
            for row in range(rows)
            for c in range(c_size)
            for r in range(r_size)
        ],
        axis=0,
    )
    dy_low = dy.astype(BF)
    do = dot_nt(dy_low, wout_ref[...]).astype(BF)
    grads = []
    for row in range(rows):
        qkv = qkv_ref[row]
        q, k, v = qkv[:, :d], qkv[:, d : 2 * d], qkv[:, 2 * d :]
        low = [p_ref[row, i] for i in range(HEADS)]
        weights = [w.astype(F32) for w in low]
        part = slice(row * length, (row + 1) * length)
        grads.append(
            jnp.concatenate(heads_back(weights, low, do[part], q, k, v, masks, factor), axis=1)
        )
    dqkv = jnp.concatenate(grads, axis=0)
    g = dot_nt(dqkv, wqkv_ref[...])
    n, inverse = norm(load_cells(x_ref, c_size, wl))
    h = (n * gain_ref[...]).astype(BF)
    dt = (dy + norm_back(g, n, inverse, gain_ref[...])).astype(BF)
    for row in range(rows):
        for s in range(c_size):
            at = row * length + s * wl
            dt_ref[s, row * wl : (row + 1) * wl] = dt[at : at + wl]
    dg_s[...] += jnp.sum(g * n, axis=0, keepdims=True)
    dwqkv_s[...] += dot_tn(h, dqkv)
    dwout_s[...] += dot_tn(jnp.concatenate([o_ref[row] for row in range(rows)], axis=0), dy_low)

    @pl.when(step == steps - 1)
    def _():
        scale = float(length * steps * rows * r_size * c_size) ** (-0.5)
        parity = lax.rem(lax.axis_index("cols"), 2)
        for i in range(3):
            grad = (dwqkv_s[:, i * d : (i + 1) * d] * scale).astype(BF)
            store_rows(keep_ref, send_ref, parity, i * d, grad)
        store_rows(keep_ref, send_ref, parity, 3 * d, (dwout_s[...] * scale).astype(BF))
        gains = jnp.concatenate(
            [dg_s[...], dgc_ref[...], dgm_ref[...], jnp.zeros((5, d), F32)], axis=0
        )
        store_rows(keep_ref, send_ref, parity, 4 * d, (gains * scale).astype(BF))


def pack_tokens_kernel(dims, x_ref, b_ref, out_ref):
    r_size, c_size, wl, cpd, length, d = dims
    cells = x_ref.shape[1]
    rpd = cells // wl
    extra = out_ref.shape[1] - cells
    lane = lax.broadcasted_iota(jnp.int32, (wl, length), 1)
    cell = lax.broadcasted_iota(jnp.int32, (wl, length), 0)
    place = (lane == cell + lax.axis_index("cols") * wl).astype(F32).astype(BF)
    spread = dot(b_ref[...], place)
    parts = length // d
    for s in range(c_size):
        out_ref[s, :cells] = x_ref[s]
        rows = [
            spread[s * rpd + i : s * rpd + i + 1, t * d : (t + 1) * d]
            for i in range(rpd)
            for t in range(parts)
        ]
        if extra > rpd * parts:
            rows.append(jnp.zeros((extra - rpd * parts, d), F32))
        out_ref[s, cells:] = jnp.concatenate(rows, axis=0).astype(BF)


def pack_cotangent_kernel(dims, ct_ref, b_ref, *out_refs):
    r_size, hl, cpd, length, d = dims
    r_at = lax.axis_index("rows")
    lane = lax.broadcasted_iota(jnp.int32, (hl, d), 1)
    cell = lax.broadcasted_iota(jnp.int32, (hl, d), 0)
    place = (lane == cell + r_at * hl).astype(F32).astype(BF)
    spread = dot_tn(b_ref[...], place)
    for s in range(r_size):
        for r in range(r_size):

            @pl.when(jnp.bitwise_xor(r_at, s) == r)
            def _():
                out_refs[s][: hl * cpd] = (
                    ct_ref[:, r * cpd : (r + 1) * cpd, :].astype(F32).reshape(hl * cpd, d).astype(BF)
                )
                rows = spread[r * cpd : (r + 1) * cpd]
                if cpd % 8:
                    rows = jnp.concatenate([rows, jnp.zeros((-cpd % 8, d), F32)], axis=0)
                out_refs[s][hl * cpd :] = rows.astype(BF)


def weight_grad_kernel(scale, n_out, *refs):
    ins, out_refs = refs[:8], refs[8 : 8 + n_out]
    sums = refs[8 + n_out :]
    step, steps = pl.program_id(0), pl.num_programs(0)
    pairs = tuple(zip(sums, ins[::2], ins[1::2]))

    @pl.when(step == 0)
    def _():
        for total, left, right in pairs:
            total[...] = dot_tn(left[...], right[...])

    @pl.when(step != 0)
    def _():
        for total, left, right in pairs:
            total[...] += dot_tn(left[...], right[...])

    @pl.when(step == steps - 1)
    def _():
        r_at = lax.axis_index("rows")
        d = sums[1].shape[0]
        block = out_refs[0].shape[0]
        sections = []
        for total in sums[:3]:
            sections += [(total, slice(0, d), slice(i, i + d)) for i in range(0, total.shape[1], d)]
        sections += [(sums[3], slice(i, i + d), slice(0, d)) for i in range(0, sums[3].shape[0], d)]
        for r in range(n_out):
            for s in range(n_out):

                @pl.when(jnp.bitwise_xor(r_at, s) == r)
                def _():
                    end = len(sections) * d
                    for at in range(0, block, d):
                        size = min(d, block - at)
                        row = r * block + at
                        while size > 0:
                            if row < end:
                                total, rows, lanes = sections[row // d]
                                skip = row % d
                                part = min(size, d - skip)
                                rows = slice(rows.start + skip, rows.start + skip + part)
                                piece = (total[rows, lanes] * scale).astype(BF)
                            else:
                                part = size
                                piece = jnp.zeros((part, d), BF)
                            to = row - r * block
                            out_refs[s][to : to + part] = piece
                            row, size = row + part, size - part


def unpack_kernel(dims, own_ref, got_ref, *out_refs):
    r_size, z_size, col_rows, row_rows, d, layout = dims
    r_at, c_at = lax.axis_index("rows"), lax.axis_index("cols")
    z_at, parity = lax.div(c_at, 2), lax.rem(c_at, 2)
    for core in range(2):
        copies = []
        for r in range(r_size):
            for z in range(z_size):
                for base, size, sections, at in (
                    (0, col_rows, layout[0], (r * 2 + core) * z_size + z),
                    (col_rows, row_rows, layout[1], (core * r_size + r) * z_size + z),
                ):
                    first = at * size
                    for start, stop, which, row0, lane0 in sections:
                        low, high = max(first, start), min(first + size, stop)
                        if low < high:
                            cut = slice(base + low - first, base + high - first)
                            to = slice(row0 + low - start, row0 + high - start)
                            copies.append((r, z, cut, which, to, slice(lane0, lane0 + d)))

        def place(source):
            for r, z, cut, which, to, lanes in copies:
                s, t = jnp.bitwise_xor(r_at, r), jnp.bitwise_xor(z_at, z)
                piece = source[s, t, cut, :].astype(F32)
                if which < 0:
                    for i in range(3):
                        out_refs[i][...] = piece[i : i + 1]
                else:
                    out_refs[which][to, lanes] = piece

        @pl.when(parity == core)
        def _():
            place(own_ref)

        @pl.when(parity != core)
        def _():
            place(got_ref)


def column_kernel(
    dims, *refs
):
    r_size, hl, cpd, length, d = dims
    y_ref, *ct_refs = refs[: 1 + r_size]
    (
        gain_ref, wqkv_ref, wout_ref, gmlp_ref, wup_ref, wdown_ref,
        dy_ref, h2_ref, dqkv_ref, o2_ref, dy2_ref, h3_ref, du_ref, act_ref, ctc_ref,
        dg_ref, dgm_ref, wire_s, x_s, ct_s, bias_s, p_s, sems, *bufs
    ) = refs[1 + r_size :]
    copies = []
    factor = float(d // HEADS) ** (-0.5)
    masks = head_masks(d)
    tokens = cpd * length

    def emit(out_ref, value):
        at = len(copies)
        bufs[at][...] = value
        copies.append(pltpu.make_async_copy(bufs[at], out_ref, sems.at[at]))
        copies[at].start()


    r_at = lax.axis_index("rows")

    for lanes in range(d // LANES):
        cut = slice(lanes * LANES, (lanes + 1) * LANES)
        wire_s[lanes] = y_ref[:, cut].astype(F32)
        for j in range(cpd):
            x_s[j, :, cut] = wire_s[lanes, pl.ds(j, length, stride=cpd), :]
    block = hl * cpd
    for lanes in range(d // LANES):
        cut = slice(lanes * LANES, (lanes + 1) * LANES)
        for s in range(r_size):
            source = jnp.bitwise_xor(r_at, s)
            to = pl.ds(pl.multiple_of(source * block, block), block)
            wire_s[lanes, to, :] = ct_refs[s][:block, cut].astype(F32)
        for j in range(cpd):
            ct_s[j, :, cut] = wire_s[lanes, pl.ds(j, length, stride=cpd), :]
    total = ct_refs[0][block:].astype(F32)
    for s in range(1, r_size):
        total = total + ct_refs[s][block:].astype(F32)
    for j in range(cpd):
        bias_s[j] = total[j : j + 1, :length]

    x = x_s[...].reshape(tokens, d)
    ct = ct_s[...].reshape(tokens, d)
    n2, r2 = norm(x)
    h2 = (n2 * gain_ref[...]).astype(BF)
    emit(h2_ref, h2)
    qkv = dot(h2, wqkv_ref[...]).astype(BF)
    outs = []
    for j in range(cpd):
        part = slice(j * length, (j + 1) * length)
        q, k, v = qkv[part, :d], qkv[part, d : 2 * d], qkv[part, 2 * d :]
        weights = softmax_heads(q, k, bias_s[j], masks, factor)
        for i in range(HEADS):
            p_s[j, i] = weights[i]
        outs.append(mix_heads([w.astype(BF) for w in weights], v, masks))
    o2 = jnp.concatenate(outs, axis=0).astype(BF)
    emit(o2_ref, o2)
    y2 = (x + dot(o2, wout_ref[...])).astype(BF).astype(F32)
    n3, r3 = norm(y2)
    h3 = (n3 * gmlp_ref[...]).astype(BF)
    emit(h3_ref, h3)
    ct_low = ct.astype(BF)
    emit(ctc_ref, ct_low)
    u = dot(h3, wup_ref[...])
    root = 0.7978845608028654
    cube = 0.044715 * root
    square = u * u
    c = 0.5 + 0.5 * jnp.tanh(u * (root + cube * square))
    emit(act_ref, (u * c).astype(BF))
    slope = c * (1.0 + (1.0 - c) * (u * (2.0 * root + 6.0 * cube * square)))
    du = (dot_nt(ct_low, wdown_ref[...]) * slope).astype(BF)
    emit(du_ref, du)
    g3 = dot_nt(du, wup_ref[...])
    dgm_ref[...] = jnp.sum(g3 * n3, axis=0, keepdims=True)
    dy2 = (ct + norm_back(g3, n3, r3, gmlp_ref[...])).astype(BF)
    emit(dy2_ref, dy2)
    do = dot_nt(dy2, wout_ref[...]).astype(BF)
    grads = []
    for j in range(cpd):
        part = slice(j * length, (j + 1) * length)
        q, k, v = qkv[part, :d], qkv[part, d : 2 * d], qkv[part, 2 * d :]
        weights = [p_s[j, i] for i in range(HEADS)]
        low = [w.astype(BF) for w in weights]
        grads.append(
            jnp.concatenate(heads_back(weights, low, do[part], q, k, v, masks, factor), axis=1)
        )
    dqkv = jnp.concatenate(grads, axis=0)
    emit(dqkv_ref, dqkv)
    g2 = dot_nt(dqkv, wqkv_ref[...])
    dg_ref[...] = jnp.sum(g2 * n2, axis=0, keepdims=True)
    dy1 = dy2.astype(F32) + norm_back(g2, n2, r2, gain_ref[...])
    x_s[...] = dy1.reshape(cpd, length, d)
    for lanes in range(d // LANES):
        cut = slice(lanes * LANES, (lanes + 1) * LANES)
        for j in range(cpd):
            wire_s[lanes, pl.ds(j, length, stride=cpd), :] = x_s[j, :, cut]
        dy_ref[:, cut] = wire_s[lanes].astype(BF)
    for copy in copies:
        copy.wait()


def whole(shape):
    return pl.BlockSpec(shape, lambda i: (0,) * len(shape))


def params():
    return pltpu.CompilerParams(
        dimension_semantics=("arbitrary",), vmem_limit_bytes=VMEM_LIMIT
    )


def whole(shape):
    return pl.BlockSpec(shape, lambda i: (0,) * len(shape))


def params():
    return pltpu.CompilerParams(
        dimension_semantics=("arbitrary",), vmem_limit_bytes=VMEM_LIMIT
    )


def row_forward(dims, rpd, recv, gain, w_qkv, w_out):
    rows = min(rpd, ROWS_FORWARD)
    r_size, c_size, wl, cpd, length, d = dims
    n_dev = r_size * c_size
    extra = recv.shape[1] - rpd * wl
    return pl.pallas_call(
        functools.partial(row_forward_kernel, dims),
        grid=(rpd // rows,),
        in_specs=[
            pl.BlockSpec((c_size, rows * wl, d), lambda i: (0, i, 0)),
            pl.BlockSpec((c_size, extra, d), lambda i: (0, rpd * wl // extra, 0)),
            whole((1, d)),
            whole((d, 3 * d)),
            whole((d, d)),
        ],
        out_specs=[
            pl.BlockSpec((n_dev, rows, cpd, d), lambda i: (0, i, 0, 0)),
            pl.BlockSpec((rows, length, 3 * d), lambda i: (i, 0, 0)),
            pl.BlockSpec((rows, length, d), lambda i: (i, 0, 0)),
            pl.BlockSpec((rows, HEADS, length, length), lambda i: (i, 0, 0, 0)),
        ],
        out_shape=[
            jax.ShapeDtypeStruct((n_dev, rpd, cpd, d), BF),
            jax.ShapeDtypeStruct((rpd, length, 3 * d), BF),
            jax.ShapeDtypeStruct((rpd, length, d), BF),
            jax.ShapeDtypeStruct((rpd, HEADS, length, length), BF),
        ],
        compiler_params=params(),
        name="row_forward",
    )(recv, recv, gain, w_qkv, w_out)


def row_backward(dims, rpd, half, recv, dy, qkv, o, p, gain, w_qkv, w_out, dg_col, dg_mlp):
    rows = min(rpd, ROWS_BACKWARD)
    r_size, c_size, wl, cpd, length, d = dims
    n_dev = r_size * c_size
    return pl.pallas_call(
        functools.partial(row_backward_kernel, dims),
        grid=(rpd // rows,),
        in_specs=[
            pl.BlockSpec((c_size, rows * wl, d), lambda i: (0, i, 0)),
            pl.BlockSpec((n_dev, rows, cpd, d), lambda i: (0, i, 0, 0)),
            pl.BlockSpec((rows, length, 3 * d), lambda i: (i, 0, 0)),
            pl.BlockSpec((rows, length, d), lambda i: (i, 0, 0)),
            pl.BlockSpec((rows, HEADS, length, length), lambda i: (i, 0, 0, 0)),
            whole((1, d)),
            whole((d, 3 * d)),
            whole((d, d)),
            whole((1, d)),
            whole((1, d)),
        ],
        out_specs=[
            pl.BlockSpec((c_size, rows * wl, d), lambda i: (0, i, 0)),
            whole((half, d)),
            whole((half, d)),
        ],
        out_shape=[
            jax.ShapeDtypeStruct((c_size, rpd * wl, d), BF),
            jax.ShapeDtypeStruct((half, d), BF),
            jax.ShapeDtypeStruct((half, d), BF),
        ],
        scratch_shapes=[
            pltpu.VMEM((1, d), F32),
            pltpu.VMEM((d, 3 * d), F32),
            pltpu.VMEM((d, d), F32),
        ],
        compiler_params=params(),
        name="row_backward",
    )(recv, dy, qkv, o, p, gain, w_qkv, w_out, dg_col, dg_mlp)


def column_stage(dims, y_wire, ct_blocks, gain, w_qkv, w_out, gain_mlp, w_up, w_down):
    r_size, hl, cpd, length, d = dims
    tokens = cpd * length
    ff = w_up.shape[1]
    widths = (d, 3 * d, d, d, d, ff, ff, d)
    order = (d, d, d, d, ff, ff, d, 3 * d)
    return pl.pallas_call(
        functools.partial(column_kernel, dims),
        out_specs=[pl.BlockSpec(memory_space=pltpu.VMEM)]
        + [pl.BlockSpec(memory_space=pl.ANY)] * len(widths)
        + [pl.BlockSpec(memory_space=pltpu.VMEM)] * 2,
        out_shape=[jax.ShapeDtypeStruct((tokens, w), BF) for w in (d,) + widths]
        + [jax.ShapeDtypeStruct((1, d), F32)] * 2,
        scratch_shapes=[
            pltpu.VMEM((d // LANES, tokens, LANES), F32),
            pltpu.VMEM((cpd, length, d), F32),
            pltpu.VMEM((cpd, length, d), F32),
            pltpu.VMEM((cpd, 1, length), F32),
            pltpu.VMEM((cpd, HEADS, length, length), F32),
            pltpu.SemaphoreType.DMA((len(order),)),
        ]
        + [pltpu.VMEM((tokens, w), BF) for w in order],
        compiler_params=pltpu.CompilerParams(vmem_limit_bytes=VMEM_LIMIT),
        name="column_stage",
    )(y_wire, *ct_blocks, gain, w_qkv, w_out, gain_mlp, w_up, w_down)


def pack_tokens(dims, extra, tokens, key_bias):
    c_size, cells, d = tokens.shape
    return pl.pallas_call(
        functools.partial(pack_tokens_kernel, dims),
        out_shape=jax.ShapeDtypeStruct((c_size, cells + extra, d), BF),
        compiler_params=pltpu.CompilerParams(vmem_limit_bytes=VMEM_LIMIT),
        name="pack_tokens",
    )(tokens, key_bias)


def pack_cotangent(dims, cotangent, key_bias):
    r_size, hl, cpd, length, d = dims
    rows = hl * cpd + cpd + -cpd % 8
    return pl.pallas_call(
        functools.partial(pack_cotangent_kernel, dims),
        out_shape=[jax.ShapeDtypeStruct((rows, d), BF)] * r_size,
        compiler_params=pltpu.CompilerParams(vmem_limit_bytes=VMEM_LIMIT),
        name="pack_cotangent",
    )(cotangent, key_bias)


def weight_grads(scale, n_out, rows, steps, pairs):
    d = pairs[1][0].shape[1]
    flat = [x for pair in pairs for x in pair]
    part = flat[0].shape[0] // steps
    return pl.pallas_call(
        functools.partial(weight_grad_kernel, scale, n_out),
        grid=(steps,),
        in_specs=[pl.BlockSpec((part, x.shape[1]), lambda i: (i, 0)) for x in flat],
        out_specs=[whole((rows // n_out, d))] * n_out,
        out_shape=[jax.ShapeDtypeStruct((rows // n_out, d), BF)] * n_out,
        scratch_shapes=[pltpu.VMEM((left.shape[1], right.shape[1]), F32) for left, right in pairs],
        compiler_params=params(),
        name="weight_grads",
    )(*flat)


def unpack(dims, own, got, shapes):
    return pl.pallas_call(
        functools.partial(unpack_kernel, dims),
        out_shape=[jax.ShapeDtypeStruct(shape, F32) for shape in shapes],
        compiler_params=pltpu.CompilerParams(vmem_limit_bytes=VMEM_LIMIT),
        name="unpack",
    )(own, got)


def exchange(x, axes):
    return lax.all_to_all(x, axes, split_axis=0, concat_axis=0, tiled=True)


def swap(x, axis, step):
    size = lax.axis_size(axis)
    return lax.ppermute(x, axis, [(i, i ^ step) for i in range(size)])


def add(parts):
    total = parts[0].astype(F32)
    for part in parts[1:]:
        total = total + part.astype(F32)
    return total.astype(BF)


def scatter_sum(blocks, axis, at, unit):
    n = blocks.shape[0]
    parts = [lax.dynamic_index_in_dim(blocks, at, 0, keepdims=False)]
    for s in range(1, n):
        block = lax.dynamic_index_in_dim(blocks, jnp.bitwise_xor(at, s), 0, keepdims=False)
        parts.append(swap(block, axis, s * unit))
    return add(parts)


def gather(block, axis, n, unit):
    return jnp.stack([block] + [swap(block, axis, s * unit) for s in range(1, n)])


def padded(rows, unit):
    return rows + -rows % unit


def shards(
    tokens, key_bias, cotangent, gain_row, w_qkv_row, w_out_row,
    gain_col, w_qkv_col, w_out_col, gain_mlp, w_up, w_down,
):
    r_size, c_size = lax.axis_size("rows"), lax.axis_size("cols")
    hl, wl, d = tokens.shape
    ff = w_up.shape[1]
    rpd, cpd = hl // c_size, wl // r_size
    row_len, col_len = wl * c_size, hl * r_size
    scale = float(row_len * col_len) ** (-0.5)
    r_at, c_at = lax.axis_index("rows"), lax.axis_index("cols")
    z_size, z_at = c_size // 2, lax.axis_index("cols") // 2
    row_dims = (r_size, c_size, wl, cpd, row_len, d)
    col_dims = (r_size, hl, cpd, col_len, d)
    unit = 8 * 2 * r_size * z_size
    col_half = padded(3 * d + d + 2 * ff, unit) // 2
    row_half = padded(4 * d + 8, unit) // 2

    extra = padded(rpd * row_len // d, 8)
    recv = exchange(
        pack_tokens(row_dims, extra, tokens.reshape(c_size, rpd * wl, d), key_bias), "cols"
    )
    ct_blocks = pack_cotangent(col_dims, cotangent, key_bias)
    ct_blocks = [ct_blocks[0]] + [swap(ct_blocks[s], "rows", s) for s in range(1, r_size)]

    y_send, qkv1, o1, p1 = row_forward(row_dims, rpd, recv, gain_row[None], w_qkv_row, w_out_row)
    y_wire = exchange(y_send, ALL).reshape(hl * r_size * cpd, d)
    (dy_send, h2, dqkv2, o2, dy2, h3, du, act, ct_cols, dg_col, dg_mlp) = column_stage(
        col_dims, y_wire, ct_blocks, gain_col[None], w_qkv_col, w_out_col,
        gain_mlp[None], w_up, w_down,
    )
    dy_wire = exchange(dy_send.reshape(y_send.shape), ALL)

    col_blocks = weight_grads(
        scale, r_size, 2 * col_half, 2, ((h2, dqkv2), (o2, dy2), (h3, du), (act, ct_cols))
    )
    col_sum = add(
        [col_blocks[0]] + [swap(col_blocks[s], "rows", s) for s in range(1, r_size)]
    )
    col_sum = scatter_sum(col_sum.reshape(2, -1, d), "cols", c_at % 2, 1)

    dt_send, keep, send = row_backward(
        row_dims, rpd, row_half, recv, dy_wire, qkv1, o1, p1, gain_row[None], w_qkv_row,
        w_out_row, dg_col, dg_mlp,
    )
    d_tokens = exchange(dt_send, "cols").reshape(hl, wl, d)
    row_sum = add([keep, swap(send, "cols", 1)])
    row_sum = scatter_sum(row_sum.reshape(r_size, -1, d), "rows", r_at, 1)
    both = jnp.concatenate(
        [col_sum.reshape(z_size, -1, d), row_sum.reshape(z_size, -1, d)], axis=1
    )
    both = scatter_sum(both, "cols", z_at, 2)
    both = gather(both, "cols", z_size, 2)
    both, d_tokens = lax.optimization_barrier((both, d_tokens))
    both = gather(both, "rows", r_size, 1)
    other = swap(both, "cols", 1)

    nff = ff // d
    col_layout = [(i * d, (i + 1) * d, 5, 0, i * d) for i in range(3)]
    col_layout += [(3 * d, 4 * d, 6, 0, 0)]
    col_layout += [((4 + i) * d, (5 + i) * d, 7, 0, i * d) for i in range(nff)]
    col_layout += [((4 + nff) * d, (4 + nff) * d + ff, 8, 0, 0)]
    row_layout = [(i * d, (i + 1) * d, 3, 0, i * d) for i in range(3)]
    row_layout += [(3 * d, 4 * d, 4, 0, 0), (4 * d, 4 * d + 8, -1, 0, 0)]
    layout = (tuple(col_layout), tuple(row_layout))
    shapes = [(1, d)] * 3 + [(d, 3 * d), (d, d), (d, 3 * d), (d, d), (d, ff), (ff, d)]
    dims = (r_size, z_size, 2 * col_half // (2 * r_size * z_size),
            2 * row_half // (2 * r_size * z_size), d, layout)
    outs = unpack(dims, both, other, shapes)
    g_row, g_col, g_mlp, qkv_row, out_row, qkv_col, out_col, up, down = outs
    return (
        d_tokens, g_row[0], qkv_row, out_row, g_col[0], qkv_col, out_col, g_mlp[0], up, down,
    )


def solution(mesh):
    cells = P("rows", "cols", None)
    in_specs = (cells, P("rows", "cols"), cells) + (P(),) * 9
    out_specs = (cells,) + (P(),) * 9
    return jax.shard_map(shards, mesh=mesh, in_specs=in_specs, out_specs=out_specs, check_vma=False)
```

```python
import functools
import jax
import jax.numpy as jnp
from jax import lax
from jax.experimental import pallas as pl
from jax.experimental.pallas import tpu as pltpu
from jax.sharding import PartitionSpec as P

HEADS = 4
LANES = 128
ALL = ("rows", "cols")
BF = jnp.bfloat16
F32 = jnp.float32
ROWS_FORWARD = 4
ROWS_BACKWARD = 2
VMEM_LIMIT = 56 * 1024 * 1024


def dot(a, b):
    return lax.dot_general(a, b, (((1,), (0,)), ((), ())), preferred_element_type=F32)


def dot_nt(a, b):
    return lax.dot_general(a, b, (((1,), (1,)), ((), ())), preferred_element_type=F32)


def dot_tn(a, b):
    return lax.dot_general(a, b, (((0,), (0,)), ((), ())), preferred_element_type=F32)


def norm(x):
    centred = x - jnp.mean(x, axis=-1, keepdims=True)
    inverse = lax.rsqrt(jnp.mean(centred * centred, axis=-1, keepdims=True) + 1e-05)
    return centred * inverse, inverse


def norm_back(grad, normed, inverse, gain):
    scaled = grad * gain
    return inverse * (
        scaled
        - jnp.mean(scaled, axis=-1, keepdims=True)
        - normed * jnp.mean(scaled * normed, axis=-1, keepdims=True)
    )


def head_masks(features):
    lane = lax.broadcasted_iota(jnp.int32, (1, features), 1) // (features // HEADS)
    return [(lane == h).astype(F32).astype(BF) for h in range(HEADS)]


def softmax_heads(q, k, bias, masks, factor):
    weights = []
    for mask in masks:
        s = dot_nt(q * (mask * factor), k) + bias
        e = jnp.exp(s - jnp.max(s, axis=-1, keepdims=True))
        weights.append(e * (1.0 / jnp.sum(e, axis=-1, keepdims=True)))
    return weights


def mix_heads(weights_low, v, masks):
    return dot(
        jnp.concatenate(weights_low, axis=1),
        jnp.concatenate([v * mask for mask in masks], axis=0),
    )


def heads_back(weights, weights_low, do, q, k, v, masks, factor):
    dos = [do * mask for mask in masks]
    low = []
    for h in range(HEADS):
        dp = dot_nt(dos[h], v)
        p = weights[h]
        centre = jnp.sum(p * dp, axis=-1, keepdims=True)
        low.append((p * (dp - centre) * factor).astype(BF))
    dq = dot(
        jnp.concatenate(low, axis=1), jnp.concatenate([k * mask for mask in masks], axis=0)
    )
    dk = dot_tn(
        jnp.concatenate(low, axis=0), jnp.concatenate([q * mask for mask in masks], axis=0)
    )
    dv = dot_tn(jnp.concatenate(weights_low, axis=0), jnp.concatenate(dos, axis=0))
    return dq.astype(BF), dk.astype(BF), dv.astype(BF)


def load_cells(ref, pieces, wl):
    rows = ref.shape[1] // wl
    return jnp.concatenate(
        [
            ref[s, i * wl : (i + 1) * wl].astype(F32)
            for i in range(rows)
            for s in range(pieces)
        ],
        axis=0,
    )


def row_bias(b_ref, row, pieces, length):
    total = b_ref[0].astype(F32)
    for s in range(1, pieces):
        total = total + b_ref[s].astype(F32)
    features = total.shape[1]
    at = lax.broadcasted_iota(jnp.int32, total.shape, 0)
    parts = length // features
    return jnp.concatenate(
        [
            jnp.sum(jnp.where(at == row * parts + t, total, 0.0), axis=0, keepdims=True)
            for t in range(parts)
        ],
        axis=1,
    )


def row_forward_kernel(
    dims, x_ref, b_ref, gain_ref, wqkv_ref, wout_ref, y_ref, qkv_ref, o_ref, p_ref
):
    r_size, c_size, wl, cpd, length, d = dims
    factor = float(d // HEADS) ** (-0.5)
    masks = head_masks(d)
    x = load_cells(x_ref, c_size, wl)
    rows = x_ref.shape[1] // wl
    n, _ = norm(x)
    h = (n * gain_ref[...]).astype(BF)
    qkv = dot(h, wqkv_ref[...]).astype(BF)
    outs = []
    for row in range(rows):
        part = slice(row * length, (row + 1) * length)
        qkv_ref[row] = qkv[part]
        q, k, v = qkv[part, :d], qkv[part, d : 2 * d], qkv[part, 2 * d :]
        bias = row_bias(b_ref, pl.program_id(0) * rows + row, c_size, length)
        low = [w.astype(BF) for w in softmax_heads(q, k, bias, masks, factor)]
        for i in range(HEADS):
            p_ref[row, i] = low[i]
        outs.append(mix_heads(low, v, masks).astype(BF))
        o_ref[row] = outs[row]
    y = (x + dot(jnp.concatenate(outs, axis=0), wout_ref[...])).astype(BF)
    for row in range(rows):
        for c in range(c_size):
            for r in range(r_size):
                at = row * length + c * wl + r * cpd
                y_ref[r * c_size + c, row] = y[at : at + cpd]


def store_rows(keep_ref, send_ref, parity, row, value):
    half = keep_ref.shape[0]
    for side in range(2):
        start, stop = max(row, side * half), min(row + value.shape[0], (side + 1) * half)
        if start < stop:
            piece = value[start - row : stop - row]
            to = slice(start - side * half, stop - side * half)

            @pl.when(parity == side)
            def _():
                keep_ref[to] = piece

            @pl.when(parity != side)
            def _():
                send_ref[to] = piece


def row_backward_kernel(
    dims, x_ref, dy_ref, qkv_ref, o_ref, p_ref, gain_ref, wqkv_ref, wout_ref, dgc_ref, dgm_ref,
    dt_ref, keep_ref, send_ref, dg_s, dwqkv_s, dwout_s,
):
    r_size, c_size, wl, cpd, length, d = dims
    step, steps = pl.program_id(0), pl.num_programs(0)
    factor = float(d // HEADS) ** (-0.5)
    masks = head_masks(d)

    @pl.when(step == 0)
    def _():
        dg_s[...] = jnp.zeros_like(dg_s)
        dwqkv_s[...] = jnp.zeros_like(dwqkv_s)
        dwout_s[...] = jnp.zeros_like(dwout_s)
        keep_ref[...] = jnp.zeros_like(keep_ref)
        send_ref[...] = jnp.zeros_like(send_ref)

    rows = dy_ref.shape[1]
    dy = jnp.concatenate(
        [
            dy_ref[r * c_size + c, row].astype(F32)
            for row in range(rows)
            for c in range(c_size)
            for r in range(r_size)
        ],
        axis=0,
    )
    dy_low = dy.astype(BF)
    do = dot_nt(dy_low, wout_ref[...]).astype(BF)
    grads = []
    for row in range(rows):
        qkv = qkv_ref[row]
        q, k, v = qkv[:, :d], qkv[:, d : 2 * d], qkv[:, 2 * d :]
        low = [p_ref[row, i] for i in range(HEADS)]
        weights = [w.astype(F32) for w in low]
        part = slice(row * length, (row + 1) * length)
        grads.append(
            jnp.concatenate(heads_back(weights, low, do[part], q, k, v, masks, factor), axis=1)
        )
    dqkv = jnp.concatenate(grads, axis=0)
    g = dot_nt(dqkv, wqkv_ref[...])
    n, inverse = norm(load_cells(x_ref, c_size, wl))
    h = (n * gain_ref[...]).astype(BF)
    dt = (dy + norm_back(g, n, inverse, gain_ref[...])).astype(BF)
    for row in range(rows):
        for s in range(c_size):
            at = row * length + s * wl
            dt_ref[s, row * wl : (row + 1) * wl] = dt[at : at + wl]
    dg_s[...] += jnp.sum(g * n, axis=0, keepdims=True)
    dwqkv_s[...] += dot_tn(h, dqkv)
    dwout_s[...] += dot_tn(jnp.concatenate([o_ref[row] for row in range(rows)], axis=0), dy_low)

    @pl.when(step == steps - 1)
    def _():
        scale = float(length * steps * rows * r_size * c_size) ** (-0.5)
        parity = lax.rem(lax.axis_index("cols"), 2)
        for i in range(3):
            grad = (dwqkv_s[:, i * d : (i + 1) * d] * scale).astype(BF)
            store_rows(keep_ref, send_ref, parity, i * d, grad)
        store_rows(keep_ref, send_ref, parity, 3 * d, (dwout_s[...] * scale).astype(BF))
        gains = jnp.concatenate(
            [dg_s[...], dgc_ref[...], dgm_ref[...], jnp.zeros((5, d), F32)], axis=0
        )
        store_rows(keep_ref, send_ref, parity, 4 * d, (gains * scale).astype(BF))


def pack_tokens_kernel(dims, x_ref, b_ref, out_ref):
    r_size, c_size, wl, cpd, length, d = dims
    cells = x_ref.shape[1]
    rpd = cells // wl
    extra = out_ref.shape[1] - cells
    lane = lax.broadcasted_iota(jnp.int32, (wl, length), 1)
    cell = lax.broadcasted_iota(jnp.int32, (wl, length), 0)
    place = (lane == cell + lax.axis_index("cols") * wl).astype(F32).astype(BF)
    spread = dot(b_ref[...], place)
    parts = length // d
    for s in range(c_size):
        out_ref[s, :cells] = x_ref[s]
        rows = [
            spread[s * rpd + i : s * rpd + i + 1, t * d : (t + 1) * d]
            for i in range(rpd)
            for t in range(parts)
        ]
        if extra > rpd * parts:
            rows.append(jnp.zeros((extra - rpd * parts, d), F32))
        out_ref[s, cells:] = jnp.concatenate(rows, axis=0).astype(BF)


def pack_cotangent_kernel(dims, ct_ref, b_ref, *out_refs):
    r_size, hl, cpd, length, d = dims
    r_at = lax.axis_index("rows")
    lane = lax.broadcasted_iota(jnp.int32, (hl, d), 1)
    cell = lax.broadcasted_iota(jnp.int32, (hl, d), 0)
    place = (lane == cell + r_at * hl).astype(F32).astype(BF)
    spread = dot_tn(b_ref[...], place)
    for s in range(r_size):
        for r in range(r_size):

            @pl.when(jnp.bitwise_xor(r_at, s) == r)
            def _():
                out_refs[s][: hl * cpd] = (
                    ct_ref[:, r * cpd : (r + 1) * cpd, :].astype(F32).reshape(hl * cpd, d).astype(BF)
                )
                rows = spread[r * cpd : (r + 1) * cpd]
                if cpd % 8:
                    rows = jnp.concatenate([rows, jnp.zeros((-cpd % 8, d), F32)], axis=0)
                out_refs[s][hl * cpd :] = rows.astype(BF)


def weight_grad_kernel(scale, n_out, *refs):
    ins, out_refs = refs[:8], refs[8 : 8 + n_out]
    sums = refs[8 + n_out :]
    step, steps = pl.program_id(0), pl.num_programs(0)
    pairs = tuple(zip(sums, ins[::2], ins[1::2]))

    @pl.when(step == 0)
    def _():
        for total, left, right in pairs:
            total[...] = dot_tn(left[...], right[...])

    @pl.when(step != 0)
    def _():
        for total, left, right in pairs:
            total[...] += dot_tn(left[...], right[...])

    @pl.when(step == steps - 1)
    def _():
        r_at = lax.axis_index("rows")
        d = sums[1].shape[0]
        block = out_refs[0].shape[0]
        sections = []
        for total in sums[:3]:
            sections += [(total, slice(0, d), slice(i, i + d)) for i in range(0, total.shape[1], d)]
        sections += [(sums[3], slice(i, i + d), slice(0, d)) for i in range(0, sums[3].shape[0], d)]
        for r in range(n_out):
            for s in range(n_out):

                @pl.when(jnp.bitwise_xor(r_at, s) == r)
                def _():
                    end = len(sections) * d
                    for at in range(0, block, d):
                        size = min(d, block - at)
                        row = r * block + at
                        while size > 0:
                            if row < end:
                                total, rows, lanes = sections[row // d]
                                skip = row % d
                                part = min(size, d - skip)
                                rows = slice(rows.start + skip, rows.start + skip + part)
                                piece = (total[rows, lanes] * scale).astype(BF)
                            else:
                                part = size
                                piece = jnp.zeros((part, d), BF)
                            to = row - r * block
                            out_refs[s][to : to + part] = piece
                            row, size = row + part, size - part


def unpack_kernel(dims, own_ref, got_ref, *refs):
    r_size, z_size, col_rows, row_rows, d, layout = dims
    *out_refs, got_s, sem = refs
    got_copy = pltpu.make_async_copy(got_ref, got_s, sem)
    got_copy.start()
    r_at, c_at = lax.axis_index("rows"), lax.axis_index("cols")
    z_at, parity = lax.div(c_at, 2), lax.rem(c_at, 2)
    halves = []
    for core in range(2):
        copies = []
        for r in range(r_size):
            for z in range(z_size):
                for base, size, sections, at in (
                    (0, col_rows, layout[0], (r * 2 + core) * z_size + z),
                    (col_rows, row_rows, layout[1], (core * r_size + r) * z_size + z),
                ):
                    first = at * size
                    for start, stop, which, row0, lane0 in sections:
                        low, high = max(first, start), min(first + size, stop)
                        if low < high:
                            cut = slice(base + low - first, base + high - first)
                            to = slice(row0 + low - start, row0 + high - start)
                            copies.append((r, z, cut, which, to, slice(lane0, lane0 + d)))
        halves.append(copies)

    def place(copies, source):
        for r, z, cut, which, to, lanes in copies:
            s, t = jnp.bitwise_xor(r_at, r), jnp.bitwise_xor(z_at, z)
            piece = source[s, t, cut, :].astype(F32)
            if which < 0:
                for i in range(3):
                    out_refs[i][...] = piece[i : i + 1]
            else:
                out_refs[which][to, lanes] = piece

    for core in range(2):

        @pl.when(parity == core)
        def _():
            place(halves[core], own_ref)

    got_copy.wait()
    for core in range(2):

        @pl.when(parity != core)
        def _():
            place(halves[core], got_s)


def column_kernel(
    dims, *refs
):
    r_size, hl, cpd, length, d = dims
    y_ref, *ct_refs = refs[: 1 + r_size]
    (
        gain_ref, wqkv_ref, wout_ref, gmlp_ref, wup_ref, wdown_ref,
        dy_ref, h2_ref, dqkv_ref, o2_ref, dy2_ref, h3_ref, du_ref, act_ref, ctc_ref,
        dg_ref, dgm_ref, wire_s, x_s, ct_s, bias_s, p_s, sems, *bufs
    ) = refs[1 + r_size :]
    copies = []
    factor = float(d // HEADS) ** (-0.5)
    masks = head_masks(d)
    tokens = cpd * length

    def emit(out_ref, value):
        at = len(copies)
        bufs[at][...] = value
        copies.append(pltpu.make_async_copy(bufs[at], out_ref, sems.at[at]))
        copies[at].start()


    r_at = lax.axis_index("rows")

    for lanes in range(d // LANES):
        cut = slice(lanes * LANES, (lanes + 1) * LANES)
        wire_s[lanes] = y_ref[:, cut].astype(F32)
        for j in range(cpd):
            x_s[j, :, cut] = wire_s[lanes, pl.ds(j, length, stride=cpd), :]
    block = hl * cpd
    for lanes in range(d // LANES):
        cut = slice(lanes * LANES, (lanes + 1) * LANES)
        for s in range(r_size):
            source = jnp.bitwise_xor(r_at, s)
            to = pl.ds(pl.multiple_of(source * block, block), block)
            wire_s[lanes, to, :] = ct_refs[s][:block, cut].astype(F32)
        for j in range(cpd):
            ct_s[j, :, cut] = wire_s[lanes, pl.ds(j, length, stride=cpd), :]
    total = ct_refs[0][block:].astype(F32)
    for s in range(1, r_size):
        total = total + ct_refs[s][block:].astype(F32)
    for j in range(cpd):
        bias_s[j] = total[j : j + 1, :length]

    x = x_s[...].reshape(tokens, d)
    ct = ct_s[...].reshape(tokens, d)
    n2, r2 = norm(x)
    h2 = (n2 * gain_ref[...]).astype(BF)
    emit(h2_ref, h2)
    qkv = dot(h2, wqkv_ref[...]).astype(BF)
    outs = []
    for j in range(cpd):
        part = slice(j * length, (j + 1) * length)
        q, k, v = qkv[part, :d], qkv[part, d : 2 * d], qkv[part, 2 * d :]
        weights = softmax_heads(q, k, bias_s[j], masks, factor)
        for i in range(HEADS):
            p_s[j, i] = weights[i]
        outs.append(mix_heads([w.astype(BF) for w in weights], v, masks))
    o2 = jnp.concatenate(outs, axis=0).astype(BF)
    emit(o2_ref, o2)
    y2 = (x + dot(o2, wout_ref[...])).astype(BF).astype(F32)
    n3, r3 = norm(y2)
    h3 = (n3 * gmlp_ref[...]).astype(BF)
    emit(h3_ref, h3)
    ct_low = ct.astype(BF)
    emit(ctc_ref, ct_low)
    u = dot(h3, wup_ref[...])
    root = 0.7978845608028654
    cube = 0.044715 * root
    square = u * u
    c = 0.5 + 0.5 * jnp.tanh(u * (root + cube * square))
    emit(act_ref, (u * c).astype(BF))
    slope = c * (1.0 + (1.0 - c) * (u * (2.0 * root + 6.0 * cube * square)))
    du = (dot_nt(ct_low, wdown_ref[...]) * slope).astype(BF)
    emit(du_ref, du)
    g3 = dot_nt(du, wup_ref[...])
    dgm_ref[...] = jnp.sum(g3 * n3, axis=0, keepdims=True)
    dy2 = (ct + norm_back(g3, n3, r3, gmlp_ref[...])).astype(BF)
    emit(dy2_ref, dy2)
    do = dot_nt(dy2, wout_ref[...]).astype(BF)
    grads = []
    for j in range(cpd):
        part = slice(j * length, (j + 1) * length)
        q, k, v = qkv[part, :d], qkv[part, d : 2 * d], qkv[part, 2 * d :]
        weights = [p_s[j, i] for i in range(HEADS)]
        low = [w.astype(BF) for w in weights]
        grads.append(
            jnp.concatenate(heads_back(weights, low, do[part], q, k, v, masks, factor), axis=1)
        )
    dqkv = jnp.concatenate(grads, axis=0)
    emit(dqkv_ref, dqkv)
    g2 = dot_nt(dqkv, wqkv_ref[...])
    dg_ref[...] = jnp.sum(g2 * n2, axis=0, keepdims=True)
    dy1 = dy2.astype(F32) + norm_back(g2, n2, r2, gain_ref[...])
    x_s[...] = dy1.reshape(cpd, length, d)
    for lanes in range(d // LANES):
        cut = slice(lanes * LANES, (lanes + 1) * LANES)
        for j in range(cpd):
            wire_s[lanes, pl.ds(j, length, stride=cpd), :] = x_s[j, :, cut]
        dy_ref[:, cut] = wire_s[lanes].astype(BF)
    for copy in copies:
        copy.wait()


def whole(shape):
    return pl.BlockSpec(shape, lambda i: (0,) * len(shape))


def params():
    return pltpu.CompilerParams(
        dimension_semantics=("arbitrary",), vmem_limit_bytes=VMEM_LIMIT
    )


def whole(shape):
    return pl.BlockSpec(shape, lambda i: (0,) * len(shape))


def params():
    return pltpu.CompilerParams(
        dimension_semantics=("arbitrary",), vmem_limit_bytes=VMEM_LIMIT
    )


def row_forward(dims, rpd, recv, gain, w_qkv, w_out):
    rows = min(rpd, ROWS_FORWARD)
    r_size, c_size, wl, cpd, length, d = dims
    n_dev = r_size * c_size
    extra = recv.shape[1] - rpd * wl
    return pl.pallas_call(
        functools.partial(row_forward_kernel, dims),
        grid=(rpd // rows,),
        in_specs=[
            pl.BlockSpec((c_size, rows * wl, d), lambda i: (0, i, 0)),
            pl.BlockSpec((c_size, extra, d), lambda i: (0, rpd * wl // extra, 0)),
            whole((1, d)),
            whole((d, 3 * d)),
            whole((d, d)),
        ],
        out_specs=[
            pl.BlockSpec((n_dev, rows, cpd, d), lambda i: (0, i, 0, 0)),
            pl.BlockSpec((rows, length, 3 * d), lambda i: (i, 0, 0)),
            pl.BlockSpec((rows, length, d), lambda i: (i, 0, 0)),
            pl.BlockSpec((rows, HEADS, length, length), lambda i: (i, 0, 0, 0)),
        ],
        out_shape=[
            jax.ShapeDtypeStruct((n_dev, rpd, cpd, d), BF),
            jax.ShapeDtypeStruct((rpd, length, 3 * d), BF),
            jax.ShapeDtypeStruct((rpd, length, d), BF),
            jax.ShapeDtypeStruct((rpd, HEADS, length, length), BF),
        ],
        compiler_params=params(),
        name="row_forward",
    )(recv, recv, gain, w_qkv, w_out)


def row_backward(dims, rpd, half, recv, dy, qkv, o, p, gain, w_qkv, w_out, dg_col, dg_mlp):
    rows = min(rpd, ROWS_BACKWARD)
    r_size, c_size, wl, cpd, length, d = dims
    n_dev = r_size * c_size
    return pl.pallas_call(
        functools.partial(row_backward_kernel, dims),
        grid=(rpd // rows,),
        in_specs=[
            pl.BlockSpec((c_size, rows * wl, d), lambda i: (0, i, 0)),
            pl.BlockSpec((n_dev, rows, cpd, d), lambda i: (0, i, 0, 0)),
            pl.BlockSpec((rows, length, 3 * d), lambda i: (i, 0, 0)),
            pl.BlockSpec((rows, length, d), lambda i: (i, 0, 0)),
            pl.BlockSpec((rows, HEADS, length, length), lambda i: (i, 0, 0, 0)),
            whole((1, d)),
            whole((d, 3 * d)),
            whole((d, d)),
            whole((1, d)),
            whole((1, d)),
        ],
        out_specs=[
            pl.BlockSpec((c_size, rows * wl, d), lambda i: (0, i, 0)),
            whole((half, d)),
            whole((half, d)),
        ],
        out_shape=[
            jax.ShapeDtypeStruct((c_size, rpd * wl, d), BF),
            jax.ShapeDtypeStruct((half, d), BF),
            jax.ShapeDtypeStruct((half, d), BF),
        ],
        scratch_shapes=[
            pltpu.VMEM((1, d), F32),
            pltpu.VMEM((d, 3 * d), F32),
            pltpu.VMEM((d, d), F32),
        ],
        compiler_params=params(),
        name="row_backward",
    )(recv, dy, qkv, o, p, gain, w_qkv, w_out, dg_col, dg_mlp)


def column_stage(dims, y_wire, ct_blocks, gain, w_qkv, w_out, gain_mlp, w_up, w_down):
    r_size, hl, cpd, length, d = dims
    tokens = cpd * length
    ff = w_up.shape[1]
    widths = (d, 3 * d, d, d, d, ff, ff, d)
    order = (d, d, d, d, ff, ff, d, 3 * d)
    return pl.pallas_call(
        functools.partial(column_kernel, dims),
        out_specs=[pl.BlockSpec(memory_space=pltpu.VMEM)]
        + [pl.BlockSpec(memory_space=pl.ANY)] * len(widths)
        + [pl.BlockSpec(memory_space=pltpu.VMEM)] * 2,
        out_shape=[jax.ShapeDtypeStruct((tokens, w), BF) for w in (d,) + widths]
        + [jax.ShapeDtypeStruct((1, d), F32)] * 2,
        scratch_shapes=[
            pltpu.VMEM((d // LANES, tokens, LANES), F32),
            pltpu.VMEM((cpd, length, d), F32),
            pltpu.VMEM((cpd, length, d), F32),
            pltpu.VMEM((cpd, 1, length), F32),
            pltpu.VMEM((cpd, HEADS, length, length), F32),
            pltpu.SemaphoreType.DMA((len(order),)),
        ]
        + [pltpu.VMEM((tokens, w), BF) for w in order],
        compiler_params=pltpu.CompilerParams(vmem_limit_bytes=VMEM_LIMIT),
        name="column_stage",
    )(y_wire, *ct_blocks, gain, w_qkv, w_out, gain_mlp, w_up, w_down)


def pack_tokens(dims, extra, tokens, key_bias):
    c_size, cells, d = tokens.shape
    return pl.pallas_call(
        functools.partial(pack_tokens_kernel, dims),
        out_shape=jax.ShapeDtypeStruct((c_size, cells + extra, d), BF),
        compiler_params=pltpu.CompilerParams(vmem_limit_bytes=VMEM_LIMIT),
        name="pack_tokens",
    )(tokens, key_bias)


def pack_cotangent(dims, cotangent, key_bias):
    r_size, hl, cpd, length, d = dims
    rows = hl * cpd + cpd + -cpd % 8
    return pl.pallas_call(
        functools.partial(pack_cotangent_kernel, dims),
        out_shape=[jax.ShapeDtypeStruct((rows, d), BF)] * r_size,
        compiler_params=pltpu.CompilerParams(vmem_limit_bytes=VMEM_LIMIT),
        name="pack_cotangent",
    )(cotangent, key_bias)


def weight_grads(scale, n_out, rows, steps, pairs):
    d = pairs[1][0].shape[1]
    flat = [x for pair in pairs for x in pair]
    part = flat[0].shape[0] // steps
    return pl.pallas_call(
        functools.partial(weight_grad_kernel, scale, n_out),
        grid=(steps,),
        in_specs=[pl.BlockSpec((part, x.shape[1]), lambda i: (i, 0)) for x in flat],
        out_specs=[whole((rows // n_out, d))] * n_out,
        out_shape=[jax.ShapeDtypeStruct((rows // n_out, d), BF)] * n_out,
        scratch_shapes=[pltpu.VMEM((left.shape[1], right.shape[1]), F32) for left, right in pairs],
        compiler_params=params(),
        name="weight_grads",
    )(*flat)


def unpack(dims, own, got, shapes):
    inside = pl.BlockSpec(memory_space=pltpu.VMEM)
    return pl.pallas_call(
        functools.partial(unpack_kernel, dims),
        in_specs=[inside, pl.BlockSpec(memory_space=pltpu.HBM)],
        out_specs=[inside] * len(shapes),
        out_shape=[jax.ShapeDtypeStruct(shape, F32) for shape in shapes],
        scratch_shapes=[pltpu.VMEM(got.shape, BF), pltpu.SemaphoreType.DMA],
        compiler_params=pltpu.CompilerParams(vmem_limit_bytes=12 * 1024 * 1024),
        name="unpack",
    )(own, got)


def exchange(x, axes):
    return lax.all_to_all(x, axes, split_axis=0, concat_axis=0, tiled=True)


def swap(x, axis, step):
    size = lax.axis_size(axis)
    return lax.ppermute(x, axis, [(i, i ^ step) for i in range(size)])


def add(parts):
    total = parts[0].astype(F32)
    for part in parts[1:]:
        total = total + part.astype(F32)
    return total.astype(BF)


def scatter_sum(blocks, axis, at, unit):
    n = blocks.shape[0]
    parts = [lax.dynamic_index_in_dim(blocks, at, 0, keepdims=False)]
    for s in range(1, n):
        block = lax.dynamic_index_in_dim(blocks, jnp.bitwise_xor(at, s), 0, keepdims=False)
        parts.append(swap(block, axis, s * unit))
    return add(parts)


def gather(block, axis, n, unit):
    return jnp.stack([block] + [swap(block, axis, s * unit) for s in range(1, n)])


def padded(rows, unit):
    return rows + -rows % unit


def shards(
    tokens, key_bias, cotangent, gain_row, w_qkv_row, w_out_row,
    gain_col, w_qkv_col, w_out_col, gain_mlp, w_up, w_down,
):
    r_size, c_size = lax.axis_size("rows"), lax.axis_size("cols")
    hl, wl, d = tokens.shape
    ff = w_up.shape[1]
    rpd, cpd = hl // c_size, wl // r_size
    row_len, col_len = wl * c_size, hl * r_size
    scale = float(row_len * col_len) ** (-0.5)
    r_at, c_at = lax.axis_index("rows"), lax.axis_index("cols")
    z_size, z_at = c_size // 2, lax.axis_index("cols") // 2
    row_dims = (r_size, c_size, wl, cpd, row_len, d)
    col_dims = (r_size, hl, cpd, col_len, d)
    unit = 8 * 2 * r_size * z_size
    col_half = padded(3 * d + d + 2 * ff, unit) // 2
    row_half = padded(4 * d + 8, unit) // 2

    extra = padded(rpd * row_len // d, 8)
    recv = exchange(
        pack_tokens(row_dims, extra, tokens.reshape(c_size, rpd * wl, d), key_bias), "cols"
    )
    ct_blocks = pack_cotangent(col_dims, cotangent, key_bias)
    ct_blocks = [ct_blocks[0]] + [swap(ct_blocks[s], "rows", s) for s in range(1, r_size)]

    y_send, qkv1, o1, p1 = row_forward(row_dims, rpd, recv, gain_row[None], w_qkv_row, w_out_row)
    y_wire = exchange(y_send, ALL).reshape(hl * r_size * cpd, d)
    (dy_send, h2, dqkv2, o2, dy2, h3, du, act, ct_cols, dg_col, dg_mlp) = column_stage(
        col_dims, y_wire, ct_blocks, gain_col[None], w_qkv_col, w_out_col,
        gain_mlp[None], w_up, w_down,
    )
    dy_wire = exchange(dy_send.reshape(y_send.shape), ALL)

    col_blocks = weight_grads(
        scale, r_size, 2 * col_half, 2, ((h2, dqkv2), (o2, dy2), (h3, du), (act, ct_cols))
    )
    col_sum = add(
        [col_blocks[0]] + [swap(col_blocks[s], "rows", s) for s in range(1, r_size)]
    )
    col_sum = scatter_sum(col_sum.reshape(2, -1, d), "cols", c_at % 2, 1)

    dt_send, keep, send = row_backward(
        row_dims, rpd, row_half, recv, dy_wire, qkv1, o1, p1, gain_row[None], w_qkv_row,
        w_out_row, dg_col, dg_mlp,
    )
    d_tokens = exchange(dt_send, "cols").reshape(hl, wl, d)
    row_sum = add([keep, swap(send, "cols", 1)])
    row_sum = scatter_sum(row_sum.reshape(r_size, -1, d), "rows", r_at, 1)
    both = jnp.concatenate(
        [col_sum.reshape(z_size, -1, d), row_sum.reshape(z_size, -1, d)], axis=1
    )
    both = scatter_sum(both, "cols", z_at, 2)
    both = gather(both, "cols", z_size, 2)
    both, d_tokens = lax.optimization_barrier((both, d_tokens))
    both = gather(both, "rows", r_size, 1)
    other = swap(both, "cols", 1)

    nff = ff // d
    col_layout = [(i * d, (i + 1) * d, 5, 0, i * d) for i in range(3)]
    col_layout += [(3 * d, 4 * d, 6, 0, 0)]
    col_layout += [((4 + i) * d, (5 + i) * d, 7, 0, i * d) for i in range(nff)]
    col_layout += [((4 + nff) * d, (4 + nff) * d + ff, 8, 0, 0)]
    row_layout = [(i * d, (i + 1) * d, 3, 0, i * d) for i in range(3)]
    row_layout += [(3 * d, 4 * d, 4, 0, 0), (4 * d, 4 * d + 8, -1, 0, 0)]
    layout = (tuple(col_layout), tuple(row_layout))
    shapes = [(1, d)] * 3 + [(d, 3 * d), (d, d), (d, 3 * d), (d, d), (d, ff), (ff, d)]
    dims = (r_size, z_size, 2 * col_half // (2 * r_size * z_size),
            2 * row_half // (2 * r_size * z_size), d, layout)
    outs = unpack(dims, both, other, shapes)
    g_row, g_col, g_mlp, qkv_row, out_row, qkv_col, out_col, up, down = outs
    return (
        d_tokens, g_row[0], qkv_row, out_row, g_col[0], qkv_col, out_col, g_mlp[0], up, down,
    )


def solution(mesh):
    cells = P("rows", "cols", None)
    in_specs = (cells, P("rows", "cols"), cells) + (P(),) * 9
    out_specs = (cells,) + (P(),) * 9
    return jax.shard_map(shards, mesh=mesh, in_specs=in_specs, out_specs=out_specs, check_vma=False)
```
